32 devices in a mesh: segment: 4 (over z), expert: 4 (over y, core), token: 2 (over x).
Axes of the slice: x: 2, y: 2, z: 4, core: 2. Of those that a mesh axis runs over, the one named last changes fastest.
Arguments:
- fwd_acts: bfloat16 [4, 256, 2048], P('segment', 'expert'), may hold values from -6 to 6
- fwd_ids: int32 [4, 256, 6], P('segment', 'expert'), may hold values from 0 to 7, as said below
- fwd_slots: int32 [4, 256, 6], P('segment', 'expert'), may hold values from 0 to 36, as said below
- bwd_acts: bfloat16 [4, 256, 2048], P('segment', 'expert'), may hold values from -6 to 6
- bwd_ids: int32 [4, 256, 6], P('segment', 'expert'), may hold values from 0 to 7, as said below
- bwd_slots: int32 [4, 256, 6], P('segment', 'expert'), may hold values from 0 to 36, as said below
- bwd_grad: bfloat16 [4, 256, 2048], P('segment', 'expert'), may hold values from -6 to 6
- norm_gain: float32 [4, 2048], P('segment'), may hold values from 0.25 to 1.75
- router: float32 [4, 2048, 8], P('segment'), may hold values from -0.125 to 0.125
- w_gate: bfloat16 [8, 2048, 1408], P('expert', None, 'token'), may hold values from -0.125 to 0.125
- w_up: bfloat16 [8, 2048, 1408], P('expert', None, 'token'), may hold values from -0.125 to 0.125
- w_down: bfloat16 [8, 1408, 2048], P('expert', 'token'), may hold values from -0.15625 to 0.15625
Outputs:
- next_acts: bfloat16 [4, 256, 2048], P('segment', 'expert', 'token')
- prev_grads: bfloat16 [4, 256, 2048], P('segment', 'expert', 'token')
The draws below stay inside these ranges and needn't reach their ends.
Inputs may be any that keep to these rules, and one draw needn't show every extreme that they name: `fwd_ids`: each row names 6 different experts. `fwd_slots`: entry (t, k) counts the assignments to expert fwd_ids[t, k] that come before it in t's block of 64 rows (rows in order, a row's 6 choices in order), capped at 36; 36 marks a dropped assignment. In every block one expert, the same for all blocks of a section, is named by more than 36 rows. `bwd_ids`: each row names 6 different experts. `bwd_slots`: entry (t, k) counts the assignments to expert bwd_ids[t, k] that come before it in t's block of 64 rows (rows in order, a row's 6 choices in order), capped at 36; 36 marks a dropped assignment. In every block one expert, the same for all blocks of a section, is named by more than 36 rows.
All inputs are finite; a program needn't handle non-finite values.
Results may differ from the reference program's by a relative error of at most 0.009.
Values may be sent and summed in bfloat16 or wider, within the bound.
A program may use at most 128 MiB of HBM per device.

```python
import jax
import jax.numpy as jnp
from jax import lax

D = 2048
FF = 1408
TOPK = 6
TOK_DEV = 64
SEGMENTS = 4
EXPERTS = 8
CAP = 36
TOKENS = 256
N_TOKEN = 2


def route_table(key):
    blocks = TOKENS // TOK_DEV
    key_hot, key_base, key_count, key_order = jax.random.split(key, 4)
    hottest = jax.random.randint(key_hot, (SEGMENTS, 1, 1, 1), 0, EXPERTS)
    columns = jnp.arange(EXPERTS, dtype=jnp.int32)
    scores = jax.random.randint(key_base, (SEGMENTS, blocks, TOK_DEV, EXPERTS), 0, 65536) * EXPERTS + columns
    counts = jax.random.randint(key_count, (SEGMENTS, blocks, 1), CAP + 1, TOK_DEV + 1)
    order_keys = jax.random.randint(key_order, (SEGMENTS, blocks, TOK_DEV), 0, 1048576) * TOK_DEV + jnp.arange(TOK_DEV, dtype=jnp.int32)
    ranking = jnp.argsort(jnp.argsort(order_keys, axis=-1), axis=-1)
    forced = ranking < counts
    scores = jnp.where(forced[..., None] & (columns == hottest), 1073741824, scores)
    _, chosen = lax.top_k(scores, TOPK)
    flattened = chosen.reshape(SEGMENTS, blocks, TOK_DEV * TOPK)
    onehot = (flattened[..., None] == columns).astype(jnp.int32)
    before = jnp.cumsum(onehot, axis=2) - onehot
    slot_ids = jnp.minimum(jnp.sum(before * onehot, axis=-1), CAP)
    return (chosen.reshape(SEGMENTS, TOKENS, TOPK).astype(jnp.int32), slot_ids.reshape(SEGMENTS, TOKENS, TOPK).astype(jnp.int32))


def draw_fwd_ids(key, part):
    return route_table(jax.random.fold_in(key, 17))[0]


def draw_fwd_slots(key, part):
    return route_table(jax.random.fold_in(key, 17))[1]


def draw_bwd_ids(key, part):
    return route_table(jax.random.fold_in(key, 29))[0]


def draw_bwd_slots(key, part):
    return route_table(jax.random.fold_in(key, 29))[1]


def steps_of(rng, extent, cuts, least, top_value):
    loudness = 1.0
    for axis_at, blocks in cuts:
        heights = jax.random.uniform(jax.random.fold_in(jax.random.fold_in(rng, 6), axis_at), (blocks,), jnp.float32, least / len(cuts), top_value / len(cuts))
        loudness = loudness * jnp.repeat(jnp.exp(heights), extent[axis_at] // blocks).reshape((-1,) + (1,) * (len(extent) - 1 - axis_at))
    return loudness


def normal_values(rng, dims, scale, most, cuts=(), kind=jnp.bfloat16):
    values = scale * jax.random.normal(rng, dims, jnp.float32)
    if cuts:
        values = values * steps_of(rng, dims, cuts, -0.22, 0.18)
    return jnp.clip(values, -most, most).astype(kind)


def setup_inputs(seed: int = 0) -> dict:
    streams_of = jax.random.split(jax.random.key(seed), 13)
    return {
        "fwd_acts": normal_values(streams_of[0], (SEGMENTS, TOKENS, D), 1.0, 6.0, ((0, 4), (1, 4))),
        "fwd_ids": draw_fwd_ids(jax.random.fold_in(streams_of[12], 71), 0),
        "fwd_slots": draw_fwd_slots(jax.random.fold_in(streams_of[12], 71), 0),
        "bwd_acts": normal_values(streams_of[3], (SEGMENTS, TOKENS, D), 1.0, 6.0, ((0, 4), (1, 4))),
        "bwd_ids": draw_bwd_ids(jax.random.fold_in(streams_of[12], 71), 0),
        "bwd_slots": draw_bwd_slots(jax.random.fold_in(streams_of[12], 71), 0),
        "bwd_grad": normal_values(streams_of[6], (SEGMENTS, TOKENS, D), 1.0, 6.0, ((0, 4), (1, 4))),
        "norm_gain": jnp.clip(1.0 + 0.15 * jax.random.normal(streams_of[7], (SEGMENTS, D), jnp.float32), 0.25, 1.75),
        "router": normal_values(streams_of[8], (SEGMENTS, D, EXPERTS), D ** -0.5, 0.125, ((0, 4),), jnp.float32),
        "w_gate": normal_values(streams_of[9], (EXPERTS, D, FF), D ** -0.5, 0.125, ((0, 4), (2, 2))),
        "w_up": normal_values(streams_of[10], (EXPERTS, D, FF), D ** -0.5, 0.125, ((0, 4), (2, 2))),
        "w_down": normal_values(streams_of[11], (EXPERTS, FF, D), FF ** -0.5, 0.15625, ((0, 4), (1, 2))),
    }


route_scale = 2.446
norm_eps = 1e-06
highest = lax.Precision.HIGHEST

def normalize(values, norm_scale):
    widened = values.astype(jnp.float32)
    inverse = lax.rsqrt(lax.optimization_barrier(jnp.mean(widened * widened, axis=-1, keepdims=True)) + norm_eps)
    scaled = widened * inverse
    return ((scaled * norm_scale).astype(jnp.bfloat16), scaled, inverse)

def gating(normed, expert_ids, router):
    logits = jnp.dot(normed.astype(jnp.float32), router, precision=highest)
    sigmoids = jax.nn.sigmoid(logits)
    picked = (expert_ids[..., None] == jnp.arange(router.shape[1], dtype=jnp.int32)).astype(jnp.float32)
    chosen = lax.optimization_barrier(jnp.sum(picked * sigmoids[..., None, :], axis=-1))
    totals = lax.optimization_barrier(jnp.sum(chosen, axis=-1, keepdims=True))
    return (route_scale * chosen / totals, chosen, totals, picked)

def finish(fwd_rows, mixed_fwd, normed_b, scaled_b, inverse_b, ids_b, cotangent, mixed_back, grad_gates, norm_scale, router):
    next_rows = (fwd_rows.astype(jnp.float32) + mixed_fwd).astype(jnp.bfloat16)
    gates_b, chosen, totals, picked = gating(normed_b, ids_b, router)
    grad_probs = route_scale * grad_gates / totals - route_scale * lax.optimization_barrier(jnp.sum(grad_gates * chosen, axis=-1, keepdims=True)) / (totals * totals)
    grad_logit = grad_probs * chosen * (1.0 - chosen)
    dense_grad = lax.optimization_barrier(jnp.sum(picked * grad_logit[..., None], axis=-2))
    grad_norm = mixed_back + jnp.dot(dense_grad, router.T, precision=highest)
    grad_scaled = grad_norm * norm_scale
    grad_in = inverse_b * (grad_scaled - scaled_b * lax.optimization_barrier(jnp.mean(grad_scaled * scaled_b, axis=-1, keepdims=True)))
    prev_rows = (cotangent.astype(jnp.float32) + grad_in).astype(jnp.bfloat16)
    return (next_rows, prev_rows)

def part_sum(pieces):
    rounded = lax.optimization_barrier(pieces.astype(jnp.bfloat16))
    return lax.optimization_barrier(jnp.sum(rounded.astype(jnp.float32), axis=0))

def expert_block(pieces):
    rows_fwd, rows_saved, rows_cot, gate_w, up_w, down_w = pieces
    count_rows = rows_fwd.shape[0]
    split_down = down_w.reshape(N_TOKEN, -1, down_w.shape[1]).astype(jnp.float32)
    split_gate_w = gate_w.reshape(gate_w.shape[0], N_TOKEN, -1).astype(jnp.float32)
    split_up_w = up_w.reshape(up_w.shape[0], N_TOKEN, -1).astype(jnp.float32)

    def down_parts(active):
        split_act = active.reshape(count_rows, N_TOKEN, -1).astype(jnp.float32)
        return part_sum(jnp.einsum('rnf,nfd->nrd', split_act, split_down, precision=highest))
    gate_fwd = jnp.dot(rows_fwd, gate_w, preferred_element_type=jnp.float32)
    up_fwd = jnp.dot(rows_fwd, up_w, preferred_element_type=jnp.float32)
    active = (gate_fwd * jax.nn.sigmoid(gate_fwd) * up_fwd).astype(jnp.bfloat16)
    out_fwd = down_parts(active)
    gate_bwd = jnp.dot(rows_saved, gate_w, preferred_element_type=jnp.float32)
    up_bwd = jnp.dot(rows_saved, up_w, preferred_element_type=jnp.float32)
    sigma = jax.nn.sigmoid(gate_bwd)
    active_bwd = (gate_bwd * sigma * up_bwd).astype(jnp.bfloat16)
    out_bwd = down_parts(active_bwd)
    grad_act = jnp.dot(rows_cot, down_w.T, preferred_element_type=jnp.float32)
    grad_gate = (grad_act * up_bwd * sigma * (1.0 + gate_bwd * (1.0 - sigma))).astype(jnp.bfloat16)
    grad_up = (grad_act * gate_bwd * sigma).astype(jnp.bfloat16)
    split_gg = grad_gate.reshape(count_rows, N_TOKEN, -1).astype(jnp.float32)
    split_gu = grad_up.reshape(count_rows, N_TOKEN, -1).astype(jnp.float32)
    back_pieces = jnp.einsum('rnf,dnf->nrd', split_gg, split_gate_w, precision=highest) + jnp.einsum('rnf,dnf->nrd', split_gu, split_up_w, precision=highest)
    back_in = part_sum(back_pieces)
    return (out_fwd, out_bwd, back_in)

def reference(fwd_acts, fwd_ids, fwd_slots, bwd_acts, bwd_ids, bwd_slots, bwd_grad, norm_gain, router, w_gate, w_up, w_down):
    blocks = TOKENS // TOK_DEV
    rows_per = blocks * CAP
    holder = EXPERTS * rows_per
    block_of = (jnp.arange(TOKENS, dtype=jnp.int32) // TOK_DEV)[:, None]

    def placing(expert_ids, slot_ids):
        return jnp.where(slot_ids < CAP, (expert_ids * blocks + block_of) * CAP + slot_ids, holder).astype(jnp.int32)

    def fill_buffer(token_rows, place):
        spread = jnp.repeat(token_rows, TOPK, axis=0)
        blank_rows = jnp.zeros((holder + 1, D), token_rows.dtype)
        filled = blank_rows.at[place.reshape(-1)].set(spread)
        return filled[:holder].reshape(EXPERTS, rows_per, D)

    def lookup(values, place):
        flattened = jnp.concatenate((values.reshape(holder, D), jnp.zeros((1, D), jnp.float32)), axis=0)
        return flattened[place]

    def segment_layer(inputs):
        fwd_x, ids_a, slots_a, bwd_x, ids_b, slots_b, cotangent, norm_scale, segment_router = inputs
        normed_a, _, _ = normalize(fwd_x, norm_scale)
        normed_b, scaled_b, inverse_b = normalize(bwd_x, norm_scale)
        place_a = placing(ids_a, slots_a)
        place_b = placing(ids_b, slots_b)
        buffer_a = fill_buffer(normed_a, place_a)
        buffer_b = fill_buffer(normed_b, place_b)
        buffer_c = fill_buffer(cotangent, place_b)
        out_fwd, out_bwd, back_in = lax.map(expert_block, (buffer_a, buffer_b, buffer_c, w_gate, w_up, w_down))
        gates_a = gating(normed_a, ids_a, segment_router)[0]
        gates_b = gating(normed_b, ids_b, segment_router)[0]
        mixed_fwd = lax.optimization_barrier(jnp.sum(gates_a[..., None] * lookup(out_fwd, place_a), axis=1))
        mixed_back = lax.optimization_barrier(jnp.sum(gates_b[..., None] * lookup(back_in, place_b), axis=1))
        grad_gates = lax.optimization_barrier(jnp.sum(cotangent.astype(jnp.float32)[:, None, :] * lookup(out_bwd, place_b), axis=-1))
        return finish(fwd_x, mixed_fwd, normed_b, scaled_b, inverse_b, ids_b, cotangent, mixed_back, grad_gates, norm_scale, segment_router)
    next_all, prev_all = lax.map(segment_layer, (fwd_acts, fwd_ids, fwd_slots, bwd_acts, bwd_ids, bwd_slots, bwd_grad, norm_gain, router))
    zero_block = jnp.zeros((1, TOKENS, D), next_all.dtype)
    next_acts = jnp.concatenate((zero_block, next_all[:-1]), axis=0)
    prev_grads = jnp.concatenate((prev_all[1:], zero_block), axis=0)
    return (next_acts, prev_grads)
```

```python
import functools

import jax
import jax.numpy as jnp
from jax import lax
from jax.experimental import pallas as pl
from jax.experimental.pallas import tpu as pltpu
from jax.sharding import PartitionSpec as P

route_scale = 2.446
norm_eps = 1e-06
highest = lax.Precision.HIGHEST
MESH = pl.DeviceIdType.MESH
f32 = jnp.float32
bf16 = jnp.bfloat16
NT = (((1,), (1,)), ((), ()))
NN = (((1,), (0,)), ((), ()))


def mm(a, b, dims=NN):
    return lax.dot_general(a, b, dims, preferred_element_type=f32)


def kernel(
    sizes,
    fa,
    ba,
    bg,
    ids_a,
    slots_a,
    ids_b,
    slots_b,
    gain_h,
    router_h,
    wg_h,
    wu_h,
    wd_h,
    out_next,
    out_prev,
    X,
    N,
    G,
    wg,
    wu,
    wd,
    act,
    gg,
    gu,
    Pb,
    R1,
    QA,
    R2A,
    ZA,
    R3A,
    QB,
    R2B,
    ZB,
    R3B,
    Sc,
    Sb,
    RS,
    DGT,
    own,
    own_base,
    zbuf,
    turn,
    table,
    gain,
    router_t,
    w_sem,
    l_sem,
    i_sem,
    s0,
    r0,
    s1,
    r1,
    sg,
    rg,
    ssib,
    rsib,
    stok,
    rtok,
    sR1,
    rR1,
    sR2A,
    rR2A,
    sR3A,
    rR3A,
    sR2B,
    rR2B,
    sR3B,
    rR3B,
    sS,
    rS,
    sz,
    rz,
):
    n_seg, n_e, n_t, per, E, tok, D, F, K, CH, cap = sizes
    J = n_e // 2
    W = D // n_t
    H = W // 2
    T = n_e * tok
    seg = lax.axis_index("segment")
    me = lax.axis_index("expert")
    x = lax.axis_index("token")
    k = lax.rem(me, 2)
    j0 = me // 2
    sib = j0 * 2 + 1 - k

    def cols(share):
        return pl.ds(pl.multiple_of(share * W, 128), W)

    first_slot = [sum(CH[:s]) for s in range(4)]

    def rows_of(s, c):
        R = tok // CH[s]
        return slice(c * R, (c + 1) * R)

    def rcopy(src, dst, ss, rs, dev):
        return pltpu.make_async_remote_copy(
            src_ref=src, dst_ref=dst, send_sem=ss, recv_sem=rs, device_id=dev, device_id_type=MESH
        )

    started = []

    def go(copy):
        copy.start()
        started.append(copy)
        return copy

    def piece(copy):
        copy.start()
        return copy

    def load(src, dst, sem):
        c = pltpu.make_async_copy(src, dst, sem)
        c.start()
        return c

    with jax.named_scope("p01_local"):
        ins = (fa, ba, bg)
        local = [load(ins[s].at[0], X.at[s, k, j0], l_sem.at[s]) for s in range(3)]
        small = [load(ref, table.at[n], i_sem.at[n]) for n, ref in enumerate((ids_a, slots_a, ids_b, slots_b))]
        small.append(load(gain_h, gain, i_sem.at[4]))
        small.append(load(router_h, router_t, i_sem.at[5]))

        barrier = pltpu.get_barrier_semaphore()
        for de in range(n_e):
            for dt in range(n_t):
                if de or dt:
                    pl.semaphore_signal(
                        barrier,
                        inc=1,
                        device_id={"expert": lax.rem(me + de, n_e), "token": lax.rem(x + dt, n_t)},
                        device_id_type=MESH,
                    )

        @pl.when(seg > 0)
        def _():
            pl.semaphore_signal(barrier, inc=1, device_id={"segment": seg - 1}, device_id_type=MESH)

        @pl.when(seg < n_seg - 1)
        def _():
            pl.semaphore_signal(barrier, inc=1, device_id={"segment": seg + 1}, device_id_type=MESH)

    with jax.named_scope("p02_barrier"):
        inner = jnp.where(seg > 0, 1, 0) + jnp.where(seg < n_seg - 1, 1, 0)
        pl.semaphore_wait(barrier, n_e * n_t - 1 + inner)

    c0 = [None] * 3
    c1 = [None] * 3

    def send_own(s):
        c1[s] = [
            [
                piece(
                    rcopy(
                        ins[s].at[0, rows_of(s, c), cols(x)],
                        X.at[s, k, j0, rows_of(s, c), cols(x)],
                        s1.at[s, d - 1],
                        r1.at[d - 1, first_slot[s] + c],
                        {"expert": lax.rem(j0 + d, J) * 2 + k},
                    )
                )
                for c in range(CH[s])
            ]
            for d in range(1, J)
        ]
        for d in range(1, J):
            whole = X.at[s, k, j0, :, cols(x)]
            started.append(rcopy(whole, whole, s1.at[s, d - 1], r1.at[d - 1, 0], {"expert": sib}))
        c0[s] = go(rcopy(ins[s].at[0], X.at[s, k, j0], s0.at[s], r0.at[s], {"expert": sib}))

    with jax.named_scope("p03_send"):
        send_own(0)
    with jax.named_scope("p04_codes"):
        weights = [[], [], []]
        pairs = [(i, e) for e in range(per) for i in (0, 1)] + [(2, e) for e in range(per)]
        for i, e in pairs:
            weights[i].append(load(((wg_h, wu_h, wd_h)[i]).at[e], (wg, wu, wd)[i].at[e], w_sem.at[i, e]))
        for c in small:
            c.wait()
        turn[...] = jnp.zeros((128, 128), f32)
        for n in range(2):
            for c in range(K):
                code = table[2 * n, c] + jnp.where(table[2 * n + 1, c] < cap, 0, E)
                turn[n * K + c : n * K + c + 1, 0:tok] = code.astype(f32)
        codes_f = jnp.transpose(turn[...])[0:tok].astype(jnp.int32)

    def normed_block(raw):
        wide = raw.astype(f32)
        inverse = lax.rsqrt(jnp.mean(wide * wide, axis=-1, keepdims=True) + norm_eps)
        scaled = wide * inverse
        return (scaled * gain[...]).astype(bf16), inverse

    lane = lax.broadcasted_iota(jnp.int32, (tok, E), 1)

    def gating(normed, first):
        logits = lax.dot_general(
            normed.astype(f32), router_t[...], NT, precision=highest, preferred_element_type=f32
        )
        probs = jax.nn.sigmoid(logits)
        picked = jnp.zeros((tok, E), f32)
        kept = jnp.zeros((tok, E), f32)
        for c in range(K):
            code = codes_f[:, first + c : first + c + 1]
            held = (code == lane).astype(f32)
            kept += held
            picked += held + (code == lane + E).astype(f32)
        total = jnp.sum(picked * probs, axis=-1, keepdims=True)
        return logits, probs, picked, kept, total, kept * (route_scale * probs / total)

    with jax.named_scope("p05_gating"):
        for c in local:
            c.wait()
        normed_a, _ = normed_block(X[0, k, j0])
        N[k, j0] = normed_a
        gates_a = gating(normed_a, 0)[5]
        normed_b, inverse_b = normed_block(X[1, k, j0])
        logits_b, probs_b, picked_b, kept_b, total_b, gates_b = gating(normed_b, K)
        own[0, :, 0:E] = logits_b
        own[1, :, 0:E] = probs_b
        own[2, :, 0:E] = picked_b
        own[3, :, 0:E] = kept_b
        own[4, :, 0:E] = jnp.broadcast_to(total_b, (tok, E))
        own[5, :, 0:E] = jnp.broadcast_to(inverse_b, (tok, E))
        G[k, j0] = jnp.zeros((tok, 128), f32)
        G[k, j0, :, 0:E] = gates_a
        G[k, j0, :, E : 2 * E] = gates_b
        cg = [
            go(
                rcopy(
                    G.at[k, j0],
                    G.at[k, j0],
                    sg.at[d - 1],
                    rg.at[d - 1],
                    {"expert": lax.rem(me + d, n_e)},
                )
            )
            for d in range(1, n_e)
        ]

        send_own(1)
        send_own(2)

    to_tok = {}
    hops = [[(d, c) for d in range(1, J) for c in range(CH[s])] for s in range(3)]

    def relay_first(s, d, c):
        src = lax.rem(j0 - d + J, J)
        c1[s][d - 1][c].wait_recv()
        part = X.at[s, k, src, rows_of(s, c), cols(x)]
        for t in range(1, n_t):
            to_tok[s, d, c, t] = piece(
                rcopy(
                    part,
                    part,
                    stok.at[s, d - 1, t - 1],
                    rtok.at[d - 1, t - 1, first_slot[s] + c],
                    {"token": lax.rem(x + t, n_t)},
                )
            )
            if c == 0:
                whole = X.at[s, k, src, :, cols(x)]
                started.append(
                    rcopy(
                        whole,
                        whole,
                        stok.at[s, d - 1, t - 1],
                        rtok.at[d - 1, t - 1, 0],
                        {"token": lax.rem(x + t, n_t)},
                    )
                )
        piece(to_sib(s, d, c, part))
        if c == 0:
            started.append(to_sib(s, d, 0, X.at[s, k, src]))

    def to_sib(s, d, c, part):
        return rcopy(
            part, part, ssib.at[s, d - 1], rsib.at[d - 1, first_slot[s] + c], {"expert": sib}
        )

    def relay_second(s, d, c):
        src = lax.rem(j0 - d + J, J)
        for t in range(1, n_t):
            to_tok[s, d, c, t].wait_recv()
            part = X.at[s, k, src, rows_of(s, c), cols(lax.rem(x - t + n_t, n_t))]
            piece(to_sib(s, d, c, part))

    def arrive(s, d, c):
        src = lax.rem(j0 - d + J, J)
        to_sib(s, d, c, X.at[s, 1 - k, src, rows_of(s, c)]).wait_recv()

    def normalize_rows(s, p, d, c):
        src = lax.rem(j0 - d + J, J)
        N[p, src, rows_of(s, c)] = normed_block(X[s, p, src, rows_of(s, c)])[0]

    M = T
    wide_lane = lax.broadcasted_iota(jnp.int32, (M, 128), 1)

    def column(s, e):
        want = s * E + me * per + e
        picked = jnp.where(wide_lane == want, G[...].reshape(M, 128), 0.0)
        return jnp.sum(picked, axis=1, keepdims=True)

    def put(ref, e, value):
        ref[e] = value.astype(bf16)

    def fwd_part(e):
        rows = N[...].reshape(M, D)
        gate = mm(rows, wg[e], NT)
        up = mm(rows, wu[e], NT)
        put(act, e, gate * jax.nn.sigmoid(gate) * up * column(0, e))

    def bwd_part(e):
        rows = N[...].reshape(M, D)
        gate = mm(rows, wg[e], NT)
        up = mm(rows, wu[e], NT)
        grad_act = mm(X[2].reshape(M, D), wd[e], NT)
        sigma = jax.nn.sigmoid(gate)
        silu = gate * sigma
        ggv = grad_act * up * sigma * (1.0 + gate * (1.0 - sigma))
        guv = grad_act * silu
        col = column(1, e)
        dg = jnp.sum(guv * up, axis=1, keepdims=True)
        corr = col * jnp.sum(ggv * gate + guv * up, axis=1, keepdims=True)
        both = jnp.where(wide_lane == e, dg, 0.0) + jnp.where(wide_lane == per, corr, 0.0)
        Sc[...] = both if e == 0 else Sc[...] + both
        put(gg, e, ggv * col)
        put(gu, e, guv * col)

    def produce(r, h, ti, emit):
        at = pl.multiple_of(lax.rem(x + ti, n_t) * W + h * H, H)
        Pb[r, h, :, ti] = emit(at).astype(bf16).reshape(2, J, tok, H)
        return go(
            rcopy(
                Pb.at[r, h, 1 - k, ti],
                R1.at[r, h, ti],
                sR1.at[r, h, ti],
                rR1.at[r, h, ti],
                {"expert": sib},
            )
        )

    def token_first(r, ti, copy):
        copy.wait_recv()
        QA[r, ti - 1] = (Pb[r, 0, k, ti].astype(f32) + R1[r, 0, ti].astype(f32)).astype(bf16)
        return go(
            rcopy(
                QA.at[r, ti - 1],
                R2A.at[r, ti - 1],
                sR2A.at[r, ti - 1],
                rR2A.at[r, ti - 1],
                {"token": lax.rem(x + ti, n_t)},
            )
        )

    def expert_first(r, ti, copy):
        copy.wait_recv()
        sent = []
        for d in range(1, J):
            jd = lax.rem(j0 + d, J)
            total = Pb[r, 1, k, ti, jd].astype(f32) + R1[r, 1, ti, jd].astype(f32)
            QB[r, d - 1, ti] = total.astype(bf16)
            sent.append(
                go(
                    rcopy(
                        QB.at[r, d - 1, ti],
                        R2B.at[r, d - 1, ti],
                        sR2B.at[r, d - 1, ti],
                        rR2B.at[r, d - 1, ti],
                        {"expert": jd * 2 + k},
                    )
                )
            )
        return sent

    def then_expert(r, first, sent):
        first.wait_recv()
        for c in sent:
            c.wait_recv()
        total = Pb[r, 0, k, 0].astype(f32) + R1[r, 0, 0].astype(f32)
        for ti in range(1, n_t):
            total += R2A[r, ti - 1].astype(f32)
        ZA[r] = total.astype(bf16)
        return [
            go(
                rcopy(
                    ZA.at[r, lax.rem(j0 + d, J)],
                    R3A.at[r, d - 1],
                    sR3A.at[r, d - 1],
                    rR3A.at[r, d - 1],
                    {"expert": lax.rem(j0 + d, J) * 2 + k},
                )
            )
            for d in range(1, J)
        ]

    def own_token(r, ti, sent):
        for c in sent:
            c.wait_recv()
        total = Pb[r, 1, k, ti, j0].astype(f32) + R1[r, 1, ti, j0].astype(f32)
        for d in range(1, J):
            total += R2B[r, d - 1, ti].astype(f32)
        return total

    def then_token(r, ti, sent):
        ZB[r, ti] = own_token(r, ti, sent).astype(bf16)
        return go(
            rcopy(
                ZB.at[r, ti],
                R3B.at[r, ti - 1],
                sR3B.at[r, ti - 1],
                rR3B.at[r, ti - 1],
                {"token": lax.rem(x + ti, n_t)},
            )
        )

    def last_a(r, sent):
        for c in sent:
            c.wait_recv()
        total = ZA[r, j0].astype(f32)
        for d in range(1, J):
            total += R3A[r, d - 1].astype(f32)
        return total

    def last_b(r, mine, sent):
        total = own_token(r, 0, mine)
        for c in sent:
            c.wait_recv()
        for ti in range(1, n_t):
            total += R3B[r, ti - 1].astype(f32)
        return total

    def half_cols(h):
        return pl.ds(pl.multiple_of(x * W + h * H, 128), H)

    def send_next(h):
        part = (0, slice(None), pl.ds(h * H, H))
        return rcopy(
            zbuf.at[part],
            out_next.at[part],
            sz.at[0, h],
            rz.at[0, h],
            {"segment": lax.rem(seg + 1, n_seg)},
        )

    def send_prev(h):
        part = (slice(None), pl.ds(h * H, H))
        return rcopy(
            zbuf.at[(1,) + part],
            out_prev.at[(0,) + part],
            sz.at[1, h],
            rz.at[1, h],
            {"segment": lax.rem(seg - 1 + n_seg, n_seg)},
        )

    def emit_fwd(at):
        total = None
        for e in range(per):
            piece = mm(act[e], wd[e, :, pl.ds(at, H)])
            total = piece if total is None else total + piece
        return total

    def emit_bwd(at):
        total = None
        for e in range(per):
            for grads, w in ((gg, wg), (gu, wu)):
                piece = mm(grads[e], w[e, :, pl.ds(at, H)])
                total = piece if total is None else total + piece
        return total

    def finish_next(h, mixed):
        rows = X[0, k, j0, :, half_cols(h)].astype(f32) + mixed
        zbuf[0, :, h * H : (h + 1) * H] = rows.astype(bf16)

        @pl.when(seg < n_seg - 1)
        def _():
            send_next(h).start()

    def produce_all(r, emit, tag):
        pa = [None] * n_t
        pb = [None] * n_t
        qa = []
        qb = [None] * n_t
        for ti in range(1, n_t):
            with jax.named_scope(f"{tag}_a{ti}"):
                pa[ti] = produce(r, 0, ti, emit)
            with jax.named_scope(f"{tag}_b{ti}"):
                pb[ti] = produce(r, 1, ti, emit)
                qa.append(token_first(r, ti, pa[ti]))
        with jax.named_scope(f"{tag}_a0"):
            pa[0] = produce(r, 0, 0, emit)
            for ti in range(1, n_t):
                qb[ti] = expert_first(r, ti, pb[ti])
        with jax.named_scope(f"{tag}_b0"):
            pb[0] = produce(r, 1, 0, emit)
        return pa[0], pb[0], qa, qb

    with jax.named_scope("p07_norm"):
        c0[0].wait_recv()
        N[1 - k, j0] = normed_block(X[0, 1 - k, j0])[0]
    with jax.named_scope("p08_relay1"):
        for d, c in hops[0]:
            relay_first(0, d, c)
    with jax.named_scope("p09_relay2"):
        for d, c in hops[0]:
            relay_second(0, d, c)
            normalize_rows(0, k, d, c)
    with jax.named_scope("p10_arrive"):
        for d, c in hops[1]:
            relay_first(1, d, c)
        for d, c in hops[0]:
            arrive(0, d, c)
            normalize_rows(0, 1 - k, d, c)

    with jax.named_scope("p11_fwd0"):
        for c in cg:
            c.wait_recv()
        weights[0][0].wait()
        weights[1][0].wait()
        fwd_part(0)
    with jax.named_scope("p12_relay"):
        for d, c in hops[1]:
            relay_second(1, d, c)
        for d, c in hops[2]:
            relay_first(2, d, c)
    with jax.named_scope("p13_fwd1"):
        for e in range(1, per):
            weights[0][e].wait()
            weights[1][e].wait()
            fwd_part(e)
        for e in range(per):
            weights[2][e].wait()
    pa, pb, qa, qb = produce_all(0, emit_fwd, "p14_prod")
    with jax.named_scope("p14z_relay"):
        for d, c in hops[2]:
            relay_second(2, d, c)
    with jax.named_scope("p15_norm"):
        c0[1].wait_recv()
        for p in range(2):
            N[p, j0] = normed_block(X[1, p, j0])[0]
        for d, c in hops[1]:
            arrive(1, d, c)
        for d in range(1, J):
            src = lax.rem(j0 - d + J, J)
            for p in range(2):
                N[p, src] = normed_block(X[1, p, src])[0]

    with jax.named_scope("p16_first"):
        qb[0] = expert_first(0, 0, pb)

    with jax.named_scope("p16b_cot"):
        c0[2].wait_recv()
        for d, c in hops[2]:
            arrive(2, d, c)
    with jax.named_scope("p17_bwd0"):
        bwd_part(0)
    with jax.named_scope("p17b_fsec"):
        za = then_expert(0, pa, qa)
        zb = [then_token(0, ti, qb[ti]) for ti in range(1, n_t)]
    with jax.named_scope("p18_bwd1"):
        for e in range(1, per):
            bwd_part(e)

    with jax.named_scope("p19_sendS"):
        flipped = jnp.transpose(Sc[...])[0:8]
        for p in range(2):
            for j in range(J):
                at = (p * J + j) * tok
                Sb[j * 2 + p] = flipped[:, at : at + tok]
        cs = []
        for de in range(n_e):
            for dt in range(n_t):
                if de or dt:
                    to = lax.rem(me + de, n_e)
                    cs.append(
                        go(
                            rcopy(
                                Sb.at[to],
                                RS.at[me, x],
                                sS.at[de, dt],
                                rS.at[de, dt],
                                {"expert": to, "token": lax.rem(x + dt, n_t)},
                            )
                        )
                    )
        RS[me, x] = Sb[me]

    pa, pb, qa, qc = produce_all(1, emit_bwd, "p20_prod")
    with jax.named_scope("p21_first"):
        qc[0] = expert_first(1, 0, pb)
    with jax.named_scope("p22_finnext"):
        finish_next(0, last_a(0, za))
        finish_next(1, last_b(0, qb[0], zb))

        @pl.when(seg == 0)
        def _():
            out_next[...] = jnp.zeros(out_next.shape, bf16)

        @pl.when(seg == n_seg - 1)
        def _():
            out_prev[...] = jnp.zeros(out_prev.shape, bf16)

    with jax.named_scope("p23_dgt"):
        for c in cs:
            c.wait_recv()
        DGT[...] = jnp.zeros(DGT.shape, f32)
        corr = jnp.zeros((1, tok), f32)
        for e in range(n_e):
            total = RS[e, 0]
            for t in range(1, n_t):
                total += RS[e, t]
            DGT[e * per : (e + 1) * per, 0:tok] = total[0:per]
            corr += total[per : per + 1]
        DGT[E : E + 1, 0:tok] = corr
        turned = jnp.transpose(DGT[...])[0:tok]
        logits_b = own[0, :, 0:E]
        probs_b = own[1, :, 0:E]
        total_b = own[4, :, 0:E]
        inverse_b = own[5, :, 0:1]
        dgates = jnp.where(own[3, :, 0:E] > 0.5, turned[:, 0:E], 0.0)
        spread = jnp.sum(dgates * probs_b, axis=-1, keepdims=True)
        dprobs = route_scale * dgates / total_b - route_scale * spread / (total_b * total_b)
        dlogits = jnp.where(own[2, :, 0:E] > 0.5, dprobs * probs_b * (1.0 - probs_b), 0.0)
        mean_all = (turned[:, E : E + 1] + jnp.sum(dlogits * logits_b, axis=-1, keepdims=True)) / D
        router_own = lax.dot_general(
            dlogits, router_t[:, cols(x)], NN, precision=highest, preferred_element_type=f32
        )
        gain_own = gain[:, cols(x)]
        scaled_own = X[1, k, j0, :, cols(x)].astype(f32) * inverse_b
        cot_own = X[2, k, j0, :, cols(x)].astype(f32)
        base = cot_own + inverse_b * (router_own * gain_own - scaled_own * mean_all)
        scale_own = inverse_b * gain_own
        own_base[0] = base
        own_base[1] = scale_own

    with jax.named_scope("p24_second"):
        zb = [then_token(1, ti, qc[ti]) for ti in range(1, n_t)]
        za = then_expert(1, pa, qa)

    def finish_prev(h, mixed):
        at = slice(h * H, (h + 1) * H)
        zbuf[1, :, at] = (own_base[0, :, at] + own_base[1, :, at] * mixed).astype(bf16)

        @pl.when(seg > 0)
        def _():
            send_prev(h).start()

    with jax.named_scope("p25_lastb"):
        finish_prev(1, last_b(1, qc[0], zb))
    with jax.named_scope("p26_lasta"):
        finish_prev(0, last_a(1, za))

    with jax.named_scope("p27_end"):
        for c in started:
            c.wait_send()

        @pl.when(seg < n_seg - 1)
        def _():
            for h in range(2):
                send_next(h).wait_send()
                send_prev(h).wait_recv()

        @pl.when(seg > 0)
        def _():
            for h in range(2):
                send_prev(h).wait_send()
                send_next(h).wait_recv()


def settle(next_in, prev_in, next_out, prev_out):
    next_out[...] = next_in[...]
    prev_out[...] = prev_in[...]


def body(
    fwd_acts,
    fwd_ids,
    fwd_slots,
    bwd_acts,
    bwd_ids,
    bwd_slots,
    bwd_grad,
    norm_gain,
    router,
    w_gate,
    w_up,
    w_down,
):
    E = router.shape[2]
    per, D, F = w_gate.shape
    n_seg = lax.axis_size("segment")
    n_e = lax.axis_size("expert")
    n_t = lax.axis_size("token")
    tok = fwd_acts.shape[1]
    K = fwd_ids.shape[2]
    cap = max(2, min(3 * tok * K // (4 * E), tok - 1))
    W = D // n_t
    J = n_e // 2
    T = n_e * tok
    V = pltpu.VMEM
    dma = pltpu.SemaphoreType.DMA
    peers = max(J - 1, 1)
    CH = tuple(max(n // peers, 1) for n in (4, 2, 1))
    toks = max(n_t - 1, 1)
    scratch = [
        V((3, 2, J, tok, D), bf16),
        V((2, J, tok, D), bf16),
        V((2, J, tok, 128), f32),
        V((per, F, D), bf16),
        V((per, F, D), bf16),
        V((per, F, D), bf16),
        V((per, T, F), bf16),
        V((per, T, F), bf16),
        V((per, T, F), bf16),
        V((2, 2, 2, n_t, J, tok, W // 2), bf16),
        V((2, 2, n_t, J, tok, W // 2), bf16),
        V((2, toks, J, tok, W // 2), bf16),
        V((2, toks, J, tok, W // 2), bf16),
        V((2, J, tok, W // 2), bf16),
        V((2, peers, tok, W // 2), bf16),
        V((2, peers, n_t, tok, W // 2), bf16),
        V((2, peers, n_t, tok, W // 2), bf16),
        V((2, n_t, tok, W // 2), bf16),
        V((2, toks, tok, W // 2), bf16),
        V((T, 128), f32),
        V((n_e, 8, tok), f32),
        V((n_e, n_t, 8, tok), f32),
        V((128, 128), f32),
        V((6, tok, 128), f32),
        V((2, tok, W), f32),
        V((2, tok, W), bf16),
        V((128, 128), f32),
        V((4, K, 1, tok), jnp.int32),
        V((1, D), f32),
        V((E, D), f32),
        dma((3, per)),
        dma((3,)),
        dma((6,)),
        dma((3,)),
        dma((3,)),
        dma((3, peers)),
        dma((peers, sum(CH))),
        dma((n_e - 1,)),
        dma((n_e - 1,)),
        dma((3, peers)),
        dma((peers, sum(CH))),
        dma((3, peers, toks)),
        dma((peers, toks, sum(CH))),
        dma((2, 2, n_t)),
        dma((2, 2, n_t)),
        dma((2, toks)),
        dma((2, toks)),
        dma((2, peers)),
        dma((2, peers)),
        dma((2, peers, n_t)),
        dma((2, peers, n_t)),
        dma((2, toks)),
        dma((2, toks)),
        dma((n_e, n_t)),
        dma((n_e, n_t)),
        dma((2, 2)),
        dma((2, 2)),
    ]
    vm = pl.BlockSpec(memory_space=pltpu.VMEM)
    hbm = pl.BlockSpec(memory_space=pltpu.HBM)
    out = jax.ShapeDtypeStruct((1, tok, W), bf16)
    sizes = (n_seg, n_e, n_t, per, E, tok, D, F, K, CH, cap)
    moved = pl.pallas_call(
        functools.partial(kernel, sizes),
        out_shape=(out, out),
        in_specs=[hbm] * 12,
        out_specs=(vm, vm),
        scratch_shapes=scratch,
        compiler_params=pltpu.CompilerParams(
            collective_id=0, has_side_effects=True, vmem_limit_bytes=60 * 1024 * 1024
        ),
        name="relay_moe",
    )(
        *(
            pltpu.with_memory_space_constraint(t, pltpu.HBM)
            for t in (
                fwd_acts,
                bwd_acts,
                bwd_grad,
                *(jnp.transpose(t, (2, 0, 1)) for t in (fwd_ids, fwd_slots, bwd_ids, bwd_slots)),
                norm_gain,
                router[0].T,
                jnp.swapaxes(w_gate, 1, 2),
                jnp.swapaxes(w_up, 1, 2),
                w_down,
            )
        )
    )
    return pl.pallas_call(
        settle, out_shape=(out, out), in_specs=[vm] * 2, out_specs=(vm, vm), name="settle",
        compiler_params=pltpu.CompilerParams(vmem_limit_bytes=2 * 1024 * 1024),
    )(*moved)


def solution(mesh):
    return jax.shard_map(
        body,
        mesh=mesh,
        in_specs=(
            P("segment", "expert", None),
            P("segment", "expert", None),
            P("segment", "expert", None),
            P("segment", "expert", None),
            P("segment", "expert", None),
            P("segment", "expert", None),
            P("segment", "expert", None),
            P("segment", None),
            P("segment", None, None),
            P("expert", None, "token"),
            P("expert", None, "token"),
            P("expert", "token", None),
        ),
        out_specs=(P("segment", "expert", "token"), P("segment", "expert", "token")),
        check_vma=False,
    )
```

```python
import functools

import jax
import jax.numpy as jnp
import numpy as np
from jax import lax
from jax.experimental import pallas as pl
from jax.experimental.pallas import tpu as pltpu
from jax.sharding import PartitionSpec as P

route_scale = 2.446
norm_eps = 1e-06
highest = lax.Precision.HIGHEST
MESH = pl.DeviceIdType.MESH
f32 = jnp.float32
bf16 = jnp.bfloat16
NT = (((1,), (1,)), ((), ()))
NN = (((1,), (0,)), ((), ()))


def mm(a, b, dims=NN):
    return lax.dot_general(a, b, dims, preferred_element_type=f32)


def kernel(
    sizes,
    fa,
    ba,
    bg,
    ids_a,
    slots_a,
    ids_b,
    slots_b,
    gain_h,
    router_h,
    wg_h,
    wu_h,
    wd_h,
    out_next,
    out_prev,
    X,
    N,
    N2,
    G,
    GT,
    wg,
    wu,
    wd,
    act,
    gg,
    gu,
    Pb,
    R1,
    QA,
    R2A,
    ZA,
    R3A,
    QB,
    R2B,
    ZB,
    R3B,
    Sc,
    Sb,
    RS,
    DGT,
    own,
    own_base,
    zbuf,
    turn,
    table,
    gain,
    router_t,
    w_sem,
    l_sem,
    i_sem,
    s0,
    r0,
    s1,
    r1,
    sg,
    rg,
    ssib,
    rsib,
    stok,
    rtok,
    sR1,
    rR1,
    sR2A,
    rR2A,
    sR3A,
    rR3A,
    sR2B,
    rR2B,
    sR3B,
    rR3B,
    sS,
    rS,
    sz,
    rz,
):
    n_seg, n_e, n_t, per, E, tok, D, F, K, CH, cap = sizes
    J = n_e // 2
    W = D // n_t
    H = W // 2
    T = n_e * tok
    seg = lax.axis_index("segment")
    me = lax.axis_index("expert")
    x = lax.axis_index("token")
    k = lax.rem(me, 2)
    j0 = me // 2
    sib = j0 * 2 + 1 - k

    def cols(share):
        return pl.ds(pl.multiple_of(share * W, 128), W)

    first_slot = [sum(CH[:s]) for s in range(4)]

    def rows_of(s, c):
        R = tok // CH[s]
        return slice(c * R, (c + 1) * R)

    def rcopy(src, dst, ss, rs, dev):
        return pltpu.make_async_remote_copy(
            src_ref=src, dst_ref=dst, send_sem=ss, recv_sem=rs, device_id=dev, device_id_type=MESH
        )

    started = []

    def go(copy):
        copy.start()
        started.append(copy)
        return copy

    def piece(copy):
        copy.start()
        return copy

    def load(src, dst, sem):
        c = pltpu.make_async_copy(src, dst, sem)
        c.start()
        return c

    with jax.named_scope("p01_local"):
        ins = (fa, ba, bg)
        local = [load(ins[s].at[0], X.at[s, k, j0], l_sem.at[0]) for s in range(3)]
        local = [pltpu.make_async_copy(X.at[:, k, j0], X.at[:, k, j0], l_sem.at[0])]
        small = [load(ref, table.at[n], i_sem.at[0]) for n, ref in enumerate((ids_a, slots_a, ids_b, slots_b))]
        small = [pltpu.make_async_copy(table, table, i_sem.at[0])]
        small.append(load(gain_h, gain, i_sem.at[1]))
        small.append(load(router_h, router_t, i_sem.at[2]))

        barrier = pltpu.get_barrier_semaphore()
        for de in range(n_e):
            for dt in range(n_t):
                if de or dt:
                    pl.semaphore_signal(
                        barrier,
                        inc=1,
                        device_id={"expert": lax.rem(me + de, n_e), "token": lax.rem(x + dt, n_t)},
                        device_id_type=MESH,
                    )

        @pl.when(seg > 0)
        def _():
            pl.semaphore_signal(barrier, inc=1, device_id={"segment": seg - 1}, device_id_type=MESH)

        @pl.when(seg < n_seg - 1)
        def _():
            pl.semaphore_signal(barrier, inc=1, device_id={"segment": seg + 1}, device_id_type=MESH)

    for c in local:
        c.wait()
    with jax.named_scope("p02_barrier"):
        inner = jnp.where(seg > 0, 1, 0) + jnp.where(seg < n_seg - 1, 1, 0)
        pl.semaphore_wait(barrier, n_e * n_t - 1 + inner)

    c0 = [None] * 3
    c1 = [None] * 3

    def send_own(s):
        c1[s] = [
            [
                piece(
                    rcopy(
                        X.at[s, k, j0, rows_of(s, c), cols(x)],
                        X.at[s, k, j0, rows_of(s, c), cols(x)],
                        s1.at[d - 1],
                        r1.at[d - 1, first_slot[s] + c],
                        {"expert": lax.rem(j0 + d, J) * 2 + k},
                    )
                )
                for c in range(CH[s])
            ]
            for d in range(1, J)
        ]
        c0[s] = piece(rcopy(X.at[s, k, j0], X.at[s, k, j0], s0.at[0], r0.at[s], {"expert": sib}))

    with jax.named_scope("p03_send"):
        send_own(0)
    with jax.named_scope("p04_codes"):
        for c in small:
            c.wait()
        turn[...] = jnp.zeros((128, 128), f32)
        for n in range(2):
            for c in range(K):
                code = table[2 * n, c] + jnp.where(table[2 * n + 1, c] < cap, 0, E)
                turn[n * K + c : n * K + c + 1, 0:tok] = code.astype(f32)
        codes_f = jnp.transpose(turn[...])[0:tok].astype(jnp.int32)

    def normed_block(raw):
        wide = raw.astype(f32)
        inverse = lax.rsqrt(jnp.mean(wide * wide, axis=-1, keepdims=True) + norm_eps)
        scaled = wide * inverse
        return (scaled * gain[...]).astype(bf16), inverse

    lane = lax.broadcasted_iota(jnp.int32, (tok, E), 1)

    def gating(normed, first):
        logits = lax.dot_general(
            normed.astype(f32), router_t[...], NT, precision=highest, preferred_element_type=f32
        )
        probs = jax.nn.sigmoid(logits)
        picked = jnp.zeros((tok, E), f32)
        kept = jnp.zeros((tok, E), f32)
        for c in range(K):
            code = codes_f[:, first + c : first + c + 1]
            held = (code == lane).astype(f32)
            kept += held
            picked += held + (code == lane + E).astype(f32)
        total = jnp.sum(picked * probs, axis=-1, keepdims=True)
        return logits, probs, picked, kept, total, kept * (route_scale * probs / total)

    with jax.named_scope("p05_gating"):
        normed_a, _ = normed_block(X[0, k, j0])
        N[k, j0] = normed_a
        gates_a = gating(normed_a, 0)[5]
        normed_b, inverse_b = normed_block(X[1, k, j0])
        N2[k, j0] = normed_b
        logits_b, probs_b, picked_b, kept_b, total_b, gates_b = gating(normed_b, K)
        own[0, :, 0:E] = logits_b
        own[1, :, 0:E] = probs_b
        own[2, :, 0:E] = picked_b
        own[3, :, 0:E] = kept_b
        own[4, :, 0:E] = jnp.broadcast_to(total_b, (tok, E))
        own[5, :, 0:E] = jnp.broadcast_to(inverse_b, (tok, E))
        turn[...] = jnp.zeros((128, 128), f32)
        turn[0:tok, 0:E] = gates_a
        turn[0:tok, E : 2 * E] = gates_b
        mine = k * J + j0
        GT[mine] = jnp.transpose(turn[...])[0 : 2 * E]
        for d in range(1, n_e):
            piece(
                rcopy(GT.at[mine], GT.at[mine], sg.at[0], rg.at[0], {"expert": lax.rem(me + d, n_e)})
            )
        blocks = GT.at[pl.ds(0, n_e - 1)]
        all_gates = rcopy(blocks, blocks, sg.at[0], rg.at[0], {"expert": sib})
        started.append(all_gates)
        send_own(1)
        send_own(2)
        weights = [[], [], []]
        pairs = [(i, e) for e in range(per) for i in (0, 1)] + [(2, e) for e in range(per)]
        for i, e in pairs:
            weights[i].append(load(((wg_h, wu_h, wd_h)[i]).at[e], (wg, wu, wd)[i].at[e], w_sem.at[i, e]))

    to_tok = {}
    hops = [[(d, c) for d in range(1, J) for c in range(CH[s])] for s in range(3)]

    def relay_first(s, d, c):
        src = lax.rem(j0 - d + J, J)
        c1[s][d - 1][c].wait_recv()
        part = X.at[s, k, src, rows_of(s, c), cols(x)]
        for t in range(1, n_t):
            to_tok[s, d, c, t] = piece(
                rcopy(
                    part,
                    part,
                    stok.at[d - 1, t - 1],
                    rtok.at[d - 1, t - 1, first_slot[s] + c],
                    {"token": lax.rem(x + t, n_t)},
                )
            )
        piece(to_sib(s, d, c, part))

    def to_sib(s, d, c, part):
        return rcopy(
            part, part, ssib.at[d - 1], rsib.at[d - 1, first_slot[s] + c], {"expert": sib}
        )

    def relay_second(s, d, c):
        src = lax.rem(j0 - d + J, J)
        for t in range(1, n_t):
            to_tok[s, d, c, t].wait_recv()
            part = X.at[s, k, src, rows_of(s, c), cols(lax.rem(x - t + n_t, n_t))]
            piece(to_sib(s, d, c, part))

    def drain(ref, ss, rs):
        started.append(rcopy(ref, ref, ss, rs, {"expert": sib}))

    drain(X.at[:, k, j0], s0.at[0], r0.at[0])
    for d in range(1, J):
        src = lax.rem(j0 - d + J, J)
        drain(X.at[:, k, j0, :, cols(x)], s1.at[d - 1], r1.at[d - 1, 0])
        drain(X.at[:, k, src], ssib.at[d - 1], rsib.at[d - 1, 0])
        for t in range(1, n_t):
            drain(X.at[:, k, src, :, cols(x)], stok.at[d - 1, t - 1], rtok.at[d - 1, t - 1, 0])
    drain(Pb.at[:, :, 1 - k], sR1.at[0], rR1.at[0, 0, 0])
    drain(QA, sR2A.at[0], rR2A.at[0, 0, 0])
    drain(ZA, sR3A.at[0], rR3A.at[0, 0])
    drain(QB, sR2B.at[0], rR2B.at[0, 0, 0])
    drain(ZB.at[:, pl.ds(1, n_t - 1)], sR3B.at[0], rR3B.at[0, 0])

    def arrive(s, d, c):
        src = lax.rem(j0 - d + J, J)
        to_sib(s, d, c, X.at[s, 1 - k, src, rows_of(s, c)]).wait_recv()

    def normalize_rows(s, p, d, c):
        src = lax.rem(j0 - d + J, J)
        N[p, src, rows_of(s, c)] = normed_block(X[s, p, src, rows_of(s, c)])[0]

    M = T
    wide_lane = lax.broadcasted_iota(jnp.int32, (M, 128), 1)

    def column(s, e):
        want = s * E + me * per + e
        picked = jnp.where(wide_lane == want, G[...].reshape(M, 128), 0.0)
        return jnp.sum(picked, axis=1, keepdims=True)

    def put(ref, e, value):
        ref[e] = value.astype(bf16)

    def fwd_part(e):
        rows = N[...].reshape(M, D)
        gate = mm(rows, wg[e], NT)
        up = mm(rows, wu[e], NT)
        put(act, e, gate * jax.nn.sigmoid(gate) * up * column(0, e))

    def bwd_part(e):
        rows = N2[...].reshape(M, D)
        gate = mm(rows, wg[e], NT)
        up = mm(rows, wu[e], NT)
        grad_act = mm(X[2].reshape(M, D), wd[e], NT)
        sigma = jax.nn.sigmoid(gate)
        silu = gate * sigma
        ggv = grad_act * up * sigma * (1.0 + gate * (1.0 - sigma))
        guv = grad_act * silu
        col = column(1, e)
        dg = jnp.sum(guv * up, axis=1, keepdims=True)
        corr = col * jnp.sum(ggv * gate + guv * up, axis=1, keepdims=True)
        both = jnp.where(wide_lane == e, dg, 0.0) + jnp.where(wide_lane == per, corr, 0.0)
        Sc[...] = both if e == 0 else Sc[...] + both
        put(gg, e, ggv * col)
        put(gu, e, guv * col)

    def produce(r, h, ti, emit):
        at = pl.multiple_of(lax.rem(x + ti, n_t) * W + h * H, H)
        Pb[r, h, :, ti] = emit(at).astype(bf16).reshape(2, J, tok, H)
        return piece(
            rcopy(
                Pb.at[r, h, 1 - k, ti],
                R1.at[r, h, ti],
                sR1.at[0],
                rR1.at[r, h, ti],
                {"expert": sib},
            )
        )

    split = J == 2

    def token_first(r, ti, copy):
        copy.wait_recv()
        QA[r, ti - 1] = (Pb[r, 0, k, ti].astype(f32) + R1[r, 0, ti].astype(f32)).astype(bf16)
        return [
            piece(
                rcopy(
                    QA.at[at],
                    R2A.at[at],
                    sR2A.at[0],
                    rR2A.at[r, ti - 1, n],
                    {"token": lax.rem(x + ti, n_t)},
                )
            )
            for n, at in enumerate(((r, ti - 1, 1 - j0), (r, ti - 1, j0)) if split else ((r, ti - 1),))
        ]

    def expert_first(r, ti, copy):
        copy.wait_recv()
        sent = []
        for d in range(1, J):
            jd = lax.rem(j0 + d, J)
            total = Pb[r, 1, k, ti, jd].astype(f32) + R1[r, 1, ti, jd].astype(f32)
            QB[r, d - 1, ti] = total.astype(bf16)
            sent.append(
                piece(
                    rcopy(
                        QB.at[r, d - 1, ti],
                        R2B.at[r, d - 1, ti],
                        sR2B.at[0],
                        rR2B.at[r, d - 1, ti],
                        {"expert": jd * 2 + k},
                    )
                )
            )
        return sent

    def first_total(r, j):
        total = Pb[r, 0, k, 0, j].astype(f32) + R1[r, 0, 0, j].astype(f32)
        for ti in range(1, n_t):
            total += R2A[r, ti - 1, j].astype(f32)
        return total

    def then_expert(r, first, sent):
        first.wait_recv()
        for c in sent:
            c[0].wait_recv()
        out = []
        for d in range(1, J):
            jd = lax.rem(j0 + d, J)
            ZA[r, d - 1] = first_total(r, jd).astype(bf16)
            out.append(
                piece(
                    rcopy(
                        ZA.at[r, d - 1],
                        R3A.at[r, d - 1],
                        sR3A.at[0],
                        rR3A.at[r, d - 1],
                        {"expert": jd * 2 + k},
                    )
                )
            )
        return out

    def own_token(r, ti, sent):
        for c in sent:
            c.wait_recv()
        total = Pb[r, 1, k, ti, j0].astype(f32) + R1[r, 1, ti, j0].astype(f32)
        for d in range(1, J):
            total += R2B[r, d - 1, ti].astype(f32)
        return total

    def then_token(r, ti, sent):
        ZB[r, ti] = own_token(r, ti, sent).astype(bf16)
        return piece(
            rcopy(
                ZB.at[r, ti],
                R3B.at[r, ti - 1],
                sR3B.at[0],
                rR3B.at[r, ti - 1],
                {"token": lax.rem(x + ti, n_t)},
            )
        )

    def last_a(r, mine, sent):
        for c in mine:
            for own_part in c[1:]:
                own_part.wait_recv()
        total = first_total(r, j0)
        for c in sent:
            c.wait_recv()
        for d in range(1, J):
            total += R3A[r, d - 1].astype(f32)
        return total

    def last_b(r, mine, sent):
        total = own_token(r, 0, mine)
        for c in sent:
            c.wait_recv()
        for ti in range(1, n_t):
            total += R3B[r, ti - 1].astype(f32)
        return total

    def half_cols(h):
        return pl.ds(pl.multiple_of(x * W + h * H, 128), H)

    def send_next(h):
        part = (0, slice(None), pl.ds(h * H, H))
        return rcopy(
            zbuf.at[part],
            out_next.at[part],
            sz.at[0, h],
            rz.at[0, h],
            {"segment": lax.rem(seg + 1, n_seg)},
        )

    def send_prev(h):
        part = (slice(None), pl.ds(h * H, H))
        return rcopy(
            zbuf.at[(1,) + part],
            out_prev.at[(0,) + part],
            sz.at[1, h],
            rz.at[1, h],
            {"segment": lax.rem(seg - 1 + n_seg, n_seg)},
        )

    def emit_fwd(at):
        total = None
        for e in range(per):
            piece = mm(act[e], wd[e, :, pl.ds(at, H)])
            total = piece if total is None else total + piece
        return total

    def emit_bwd(at):
        total = None
        for e in range(per):
            for grads, w in ((gg, wg), (gu, wu)):
                piece = mm(grads[e], w[e, :, pl.ds(at, H)])
                total = piece if total is None else total + piece
        return total

    def finish_next(h, mixed):
        rows = X[0, k, j0, :, half_cols(h)].astype(f32) + mixed
        zbuf[0, :, h * H : (h + 1) * H] = rows.astype(bf16)

        @pl.when(seg < n_seg - 1)
        def _():
            send_next(h).start()

    order = [*range(1, n_t), 0]

    def produce_all(r, emit, tag):
        pa = [None] * n_t
        pb = [None] * n_t
        qa = []
        qb = [None] * n_t
        for ti in range(1, n_t):
            with jax.named_scope(f"{tag}_a{ti}"):
                pa[ti] = produce(r, 0, ti, emit)
            with jax.named_scope(f"{tag}_b{ti}"):
                pb[ti] = produce(r, 1, ti, emit)
                qa.append(token_first(r, ti, pa[ti]))
        with jax.named_scope(f"{tag}_a0"):
            pa[0] = produce(r, 0, 0, emit)
            for ti in range(1, n_t):
                qb[ti] = expert_first(r, ti, pb[ti])
        with jax.named_scope(f"{tag}_b0"):
            pb[0] = produce(r, 1, 0, emit)
        return pa[0], pb[0], qa, qb

    with jax.named_scope("p07_norm"):
        c0[0].wait_recv()
        N[1 - k, j0] = normed_block(X[0, 1 - k, j0])[0]
    with jax.named_scope("p08_relay1"):
        for d, c in hops[0]:
            relay_first(0, d, c)
    with jax.named_scope("p09_relay2"):
        for d, c in hops[0]:
            relay_second(0, d, c)
            normalize_rows(0, k, d, c)
    with jax.named_scope("p10_arrive"):
        for d, c in hops[1]:
            relay_first(1, d, c)
        c0[1].wait_recv()
        N2[1 - k, j0] = normed_block(X[1, 1 - k, j0])[0]
        for d, c in hops[0]:
            arrive(0, d, c)
            normalize_rows(0, 1 - k, d, c)

    with jax.named_scope("p11_fwd0"):
        all_gates.wait_recv()
        turn[...] = jnp.zeros((128, 128), f32)
        for p in range(2):
            for j in range(J):
                turn[0 : 2 * E] = GT[p * J + j]
                G[p, j] = jnp.transpose(turn[...])[0:tok]
        weights[0][0].wait()
        weights[1][0].wait()
        fwd_part(0)
    with jax.named_scope("p12_relay"):
        for d, c in hops[2]:
            relay_first(2, d, c)
    with jax.named_scope("p13_fwd1"):
        for e in range(1, per):
            weights[0][e].wait()
            weights[1][e].wait()
            fwd_part(e)
        for e in range(per):
            weights[2][e].wait()
    with jax.named_scope("p13b_relay"):
        for d, c in hops[1]:
            relay_second(1, d, c)
    with jax.named_scope("p14_prod"):
        pa = [produce(0, 0, ti, emit_fwd) for ti in order]
        pb = [produce(0, 1, ti, emit_fwd) for ti in order[:-1]]
        for d, c in hops[1]:
            arrive(1, d, c)
        for d in range(1, J):
            src = lax.rem(j0 - d + J, J)
            for p in range(2):
                N2[p, src] = normed_block(X[1, p, src])[0]
        pb.append(produce(0, 1, 0, emit_fwd))
    with jax.named_scope("p14z_relay"):
        for d, c in hops[2]:
            relay_second(2, d, c)
    with jax.named_scope("p16_first"):
        qa = [token_first(0, ti, pa[n]) for n, ti in enumerate(order[:-1])]
        qb = [None] * n_t
        for n, ti in enumerate(order[:-1]):
            qb[ti] = expert_first(0, ti, pb[n])
    with jax.named_scope("p16b_cot"):
        c0[2].wait_recv()
        for d, c in hops[2]:
            arrive(2, d, c)
    with jax.named_scope("p17_bwd"):
        for e in range(per):
            bwd_part(e)
    with jax.named_scope("p18_fsec"):
        za = then_expert(0, pa[-1], qa)
        zb = [then_token(0, ti, qb[ti]) for ti in range(1, n_t)]
        qb[0] = expert_first(0, 0, pb[-1])

    with jax.named_scope("p19_sendS"):
        flipped = jnp.transpose(Sc[...])[0:8]
        for p in range(2):
            for j in range(J):
                at = (p * J + j) * tok
                Sb[j * 2 + p] = flipped[:, at : at + tok]
        for de in range(n_e):
            for dt in range(n_t):
                if de or dt:
                    to = lax.rem(me + de, n_e)
                    piece(
                        rcopy(
                            Sb.at[to],
                            RS.at[me * n_t + x],
                            sS.at[0],
                            rS.at[0],
                            {"expert": to, "token": lax.rem(x + dt, n_t)},
                        )
                    )
        blocks = RS.at[pl.ds(0, n_e * n_t - 1)]
        all_sums = rcopy(blocks, blocks, sS.at[0], rS.at[0], {"expert": sib})
        started.append(all_sums)
        RS[me * n_t + x] = Sb[me]

    qa0, zb0 = qa, zb
    pa, pb, qa, qc = produce_all(1, emit_bwd, "p20_prod")
    with jax.named_scope("p21_first"):
        zc = then_expert(1, pa, qa)
    with jax.named_scope("p23_dgt"):
        all_sums.wait_recv()
        DGT[...] = jnp.zeros(DGT.shape, f32)
        corr = jnp.zeros((1, tok), f32)
        for e in range(n_e):
            total = RS[e * n_t]
            for t in range(1, n_t):
                total += RS[e * n_t + t]
            DGT[e * per : (e + 1) * per, 0:tok] = total[0:per]
            corr += total[per : per + 1]
        DGT[E : E + 1, 0:tok] = corr
        turned = jnp.transpose(DGT[...])[0:tok]
        logits_b = own[0, :, 0:E]
        probs_b = own[1, :, 0:E]
        total_b = own[4, :, 0:E]
        inverse_b = own[5, :, 0:1]
        dgates = jnp.where(own[3, :, 0:E] > 0.5, turned[:, 0:E], 0.0)
        spread = jnp.sum(dgates * probs_b, axis=-1, keepdims=True)
        dprobs = route_scale * dgates / total_b - route_scale * spread / (total_b * total_b)
        dlogits = jnp.where(own[2, :, 0:E] > 0.5, dprobs * probs_b * (1.0 - probs_b), 0.0)
        mean_all = (turned[:, E : E + 1] + jnp.sum(dlogits * logits_b, axis=-1, keepdims=True)) / D
        router_own = lax.dot_general(
            dlogits, router_t[:, cols(x)], NN, precision=highest, preferred_element_type=f32
        )
        gain_own = gain[:, cols(x)]
        scaled_own = X[1, k, j0, :, cols(x)].astype(f32) * inverse_b
        cot_own = X[2, k, j0, :, cols(x)].astype(f32)
        base = cot_own + inverse_b * (router_own * gain_own - scaled_own * mean_all)
        scale_own = inverse_b * gain_own
        own_base[0] = base
        own_base[1] = scale_own
        qc[0] = expert_first(1, 0, pb)

    with jax.named_scope("p24_second"):
        zb = [then_token(1, ti, qc[ti]) for ti in range(1, n_t)]

    with jax.named_scope("p22_finnext"):
        finish_next(0, last_a(0, qa0, za))
        finish_next(1, last_b(0, qb[0], zb0))

        @pl.when(seg == 0)
        def _():
            out_next[...] = jnp.zeros(out_next.shape, bf16)

        @pl.when(seg == n_seg - 1)
        def _():
            out_prev[...] = jnp.zeros(out_prev.shape, bf16)

    def finish_prev(h, mixed):
        at = slice(h * H, (h + 1) * H)
        zbuf[1, :, at] = (own_base[0, :, at] + own_base[1, :, at] * mixed).astype(bf16)

        @pl.when(seg > 0)
        def _():
            send_prev(h).start()

    with jax.named_scope("p25_lasta"):
        finish_prev(0, last_a(1, qa, zc))
    with jax.named_scope("p26_lastb"):
        finish_prev(1, last_b(1, qc[0], zb))

    with jax.named_scope("p27_end"):
        for c in started:
            c.wait_send()

        @pl.when(seg < n_seg - 1)
        def _():
            for h in range(2):
                send_next(h).wait_send()
                send_prev(h).wait_recv()

        @pl.when(seg > 0)
        def _():
            for h in range(2):
                send_prev(h).wait_send()
                send_next(h).wait_recv()


def settle(next_in, prev_in, next_out, prev_out):
    next_out[...] = next_in[...]
    prev_out[...] = prev_in[...]


def body(
    fwd_acts,
    fwd_ids,
    fwd_slots,
    bwd_acts,
    bwd_ids,
    bwd_slots,
    bwd_grad,
    norm_gain,
    router,
    w_gate,
    w_up,
    w_down,
):
    E = router.shape[2]
    per, D, F = w_gate.shape
    n_seg = lax.axis_size("segment")
    n_e = lax.axis_size("expert")
    n_t = lax.axis_size("token")
    tok = fwd_acts.shape[1]
    K = fwd_ids.shape[2]
    cap = max(2, min(3 * tok * K // (4 * E), tok - 1))
    W = D // n_t
    J = n_e // 2
    T = n_e * tok
    V = pltpu.VMEM
    dma = pltpu.SemaphoreType.DMA
    peers = max(J - 1, 1)
    CH = tuple(max(n // peers, 1) for n in (4, 2, 1))
    toks = max(n_t - 1, 1)
    scratch = [
        V((3, 2, J, tok, D), bf16),
        V((2, J, tok, D), bf16),
        V((2, J, tok, D), bf16),
        V((2, J, tok, 128), f32),
        V((n_e, 2 * E, 128), f32),
        V((per, F, D), bf16),
        V((per, F, D), bf16),
        V((per, F, D), bf16),
        V((per, T, F), bf16),
        V((per, T, F), bf16),
        V((per, T, F), bf16),
        V((2, 2, 2, n_t, J, tok, W // 2), bf16),
        V((2, 2, n_t, J, tok, W // 2), bf16),
        V((2, toks, J, tok, W // 2), bf16),
        V((2, toks, J, tok, W // 2), bf16),
        V((2, peers, tok, W // 2), bf16),
        V((2, peers, tok, W // 2), bf16),
        V((2, peers, n_t, tok, W // 2), bf16),
        V((2, peers, n_t, tok, W // 2), bf16),
        V((2, n_t, tok, W // 2), bf16),
        V((2, toks, tok, W // 2), bf16),
        V((T, 128), f32),
        V((n_e, 8, tok), f32),
        V((n_e * n_t, 8, tok), f32),
        V((128, 128), f32),
        V((6, tok, 128), f32),
        V((2, tok, W), f32),
        V((2, tok, W), bf16),
        V((128, 128), f32),
        V((4, K, 1, tok), jnp.int32),
        V((1, D), f32),
        V((E, D), f32),
        dma((3, per)),
        dma((1,)),
        dma((3,)),
        dma((1,)),
        dma((3,)),
        dma((peers,)),
        dma((peers, sum(CH))),
        dma((1,)),
        dma((1,)),
        dma((peers,)),
        dma((peers, sum(CH))),
        dma((peers, toks)),
        dma((peers, toks, sum(CH))),
        dma((1,)),
        dma((2, 2, n_t)),
        dma((1,)),
        dma((2, toks, 2)),
        dma((1,)),
        dma((2, peers)),
        dma((1,)),
        dma((2, peers, n_t)),
        dma((1,)),
        dma((2, toks)),
        dma((1,)),
        dma((1,)),
        dma((2, 2)),
        dma((2, 2)),
    ]
    held = sum(
        int(np.prod(s.shape)) * jnp.dtype(s.dtype).itemsize
        for s in scratch
        if s.memory_space == V
    )
    vm = pl.BlockSpec(memory_space=pltpu.VMEM)
    hbm = pl.BlockSpec(memory_space=pltpu.HBM)
    out = jax.ShapeDtypeStruct((1, tok, W), bf16)
    sizes = (n_seg, n_e, n_t, per, E, tok, D, F, K, CH, cap)
    moved = pl.pallas_call(
        functools.partial(kernel, sizes),
        out_shape=(out, out),
        in_specs=[hbm] * 12,
        out_specs=(vm, vm),
        scratch_shapes=scratch,
        compiler_params=pltpu.CompilerParams(
            collective_id=0, has_side_effects=True, vmem_limit_bytes=held + 9 * 1024 * 1024
        ),
        name="relay_moe",
    )(
        *(
            pltpu.with_memory_space_constraint(t, pltpu.HBM)
            for t in (
                fwd_acts,
                bwd_acts,
                bwd_grad,
                *(jnp.transpose(t, (2, 0, 1)) for t in (fwd_ids, fwd_slots, bwd_ids, bwd_slots)),
                norm_gain,
                router[0].T,
                jnp.swapaxes(w_gate, 1, 2),
                jnp.swapaxes(w_up, 1, 2),
                w_down,
            )
        )
    )
    return pl.pallas_call(
        settle, out_shape=(out, out), in_specs=[vm] * 2, out_specs=(vm, vm), name="settle",
        compiler_params=pltpu.CompilerParams(vmem_limit_bytes=2 * 1024 * 1024),
    )(*moved)


def solution(mesh):
    return jax.shard_map(
        body,
        mesh=mesh,
        in_specs=(
            P("segment", "expert", None),
            P("segment", "expert", None),
            P("segment", "expert", None),
            P("segment", "expert", None),
            P("segment", "expert", None),
            P("segment", "expert", None),
            P("segment", "expert", None),
            P("segment", None),
            P("segment", None, None),
            P("expert", None, "token"),
            P("expert", None, "token"),
            P("expert", "token", None),
        ),
        out_specs=(P("segment", "expert", "token"), P("segment", "expert", "token")),
        check_vma=False,
    )
```

```python
import functools

import jax
import jax.numpy as jnp
import numpy as np
from jax import lax
from jax.experimental import pallas as pl
from jax.experimental.pallas import tpu as pltpu
from jax.sharding import PartitionSpec as P

route_scale = 2.446
norm_eps = 1e-06
highest = lax.Precision.HIGHEST
MESH = pl.DeviceIdType.MESH
f32 = jnp.float32
bf16 = jnp.bfloat16
NT = (((1,), (1,)), ((), ()))
NN = (((1,), (0,)), ((), ()))


def mm(a, b, dims=NN):
    return lax.dot_general(a, b, dims, preferred_element_type=f32)


def kernel(
    sizes,
    fa,
    ba,
    bg,
    ids_a,
    slots_a,
    ids_b,
    slots_b,
    gain_h,
    router_h,
    wg_h,
    wu_h,
    wd_h,
    out_next,
    out_prev,
    X,
    N,
    N2,
    G,
    GT,
    wg,
    wu,
    wd,
    act,
    gg,
    gu,
    Pb,
    R1,
    QA,
    R2A,
    ZA,
    R3A,
    QB,
    R2B,
    ZB,
    R3B,
    Sc,
    Sb,
    RS,
    DGT,
    own,
    own_base,
    zbuf,
    turn,
    table,
    gain,
    router_t,
    w_sem,
    l_sem,
    i_sem,
    s0,
    r0,
    s1,
    r1,
    r1t,
    sg,
    rg,
    ssib,
    rsib,
    rsibt,
    stok,
    rtok,
    sR1,
    rR1,
    sR2A,
    rR2A,
    sR3A,
    rR3A,
    sR2B,
    rR2B,
    sR3B,
    rR3B,
    sS,
    rS,
    sz,
    rz,
):
    n_seg, n_e, n_t, per, E, tok, D, F, K, CH, cap = sizes
    J = n_e // 2
    W = D // n_t
    H = W // 2
    T = n_e * tok
    seg = lax.axis_index("segment")
    me = lax.axis_index("expert")
    x = lax.axis_index("token")
    k = lax.rem(me, 2)
    j0 = me // 2
    sib = j0 * 2 + 1 - k

    def cols(share):
        return pl.ds(pl.multiple_of(share * W, 128), W)

    Q = W // 4 if n_t == 2 and W % 512 == 0 else 0
    L = W - Q

    def lead(share):
        return pl.ds(pl.multiple_of(share * W, 128), L)

    def trail(share):
        return pl.ds(pl.multiple_of(share * W + L, 128), Q)

    first_slot = [sum(CH[:s]) for s in range(4)]

    def rows_of(s, c):
        R = tok // CH[s]
        return slice(c * R, (c + 1) * R)

    def rcopy(src, dst, ss, rs, dev):
        return pltpu.make_async_remote_copy(
            src_ref=src, dst_ref=dst, send_sem=ss, recv_sem=rs, device_id=dev, device_id_type=MESH
        )

    started = []

    def go(copy):
        copy.start()
        started.append(copy)
        return copy

    def piece(copy):
        copy.start()
        return copy

    def load(src, dst, sem):
        c = pltpu.make_async_copy(src, dst, sem)
        c.start()
        return c

    with jax.named_scope("p01_local"):
        ins = (fa, ba, bg)
        local = [load(ins[s].at[0], X.at[s, k, j0], l_sem.at[0]) for s in range(3)]
        local = [pltpu.make_async_copy(X.at[:, k, j0], X.at[:, k, j0], l_sem.at[0])]
        small = [load(ref, table.at[n], i_sem.at[0]) for n, ref in enumerate((ids_a, slots_a, ids_b, slots_b))]
        small = [pltpu.make_async_copy(table, table, i_sem.at[0])]
        small.append(load(gain_h, gain, i_sem.at[1]))
        small.append(load(router_h, router_t, i_sem.at[2]))

        barrier = pltpu.get_barrier_semaphore()
        for de in range(n_e):
            for dt in range(n_t):
                if de or dt:
                    pl.semaphore_signal(
                        barrier,
                        inc=1,
                        device_id={"expert": lax.rem(me + de, n_e), "token": lax.rem(x + dt, n_t)},
                        device_id_type=MESH,
                    )

        @pl.when(seg > 0)
        def _():
            pl.semaphore_signal(barrier, inc=1, device_id={"segment": seg - 1}, device_id_type=MESH)

        @pl.when(seg < n_seg - 1)
        def _():
            pl.semaphore_signal(barrier, inc=1, device_id={"segment": seg + 1}, device_id_type=MESH)

    for c in local:
        c.wait()
    with jax.named_scope("p02_barrier"):
        inner = jnp.where(seg > 0, 1, 0) + jnp.where(seg < n_seg - 1, 1, 0)
        pl.semaphore_wait(barrier, n_e * n_t - 1 + inner)

    c0 = [None] * 3
    c1 = [None] * 3

    def send_own(s):
        c1[s] = [
            [
                piece(
                    rcopy(
                        X.at[s, k, j0, rows_of(s, c), lead(x)],
                        X.at[s, k, j0, rows_of(s, c), lead(x)],
                        s1.at[d - 1],
                        r1.at[d - 1, first_slot[s] + c],
                        {"expert": lax.rem(j0 + d, J) * 2 + k},
                    )
                )
                for c in range(CH[s])
            ]
            for d in range(1, J)
        ]

    def send_rest(s):
        for d in range(1, J):
            for share in range(2 if Q else 0):
                part = X.at[s, k, j0, :, trail(share)]
                to = {"expert": lax.rem(j0 + d, J) * 2 + k}
                piece(rcopy(part, part, s1.at[d - 1], r1t.at[d - 1, s], to))
        c0[s] = piece(rcopy(X.at[s, k, j0], X.at[s, k, j0], s0.at[0], r0.at[s], {"expert": sib}))

    with jax.named_scope("p03_send"):
        send_own(0)
        send_rest(0)
    with jax.named_scope("p04_codes"):
        for c in small:
            c.wait()
        turn[...] = jnp.zeros((128, 128), f32)
        for n in range(2):
            for c in range(K):
                code = table[2 * n, c] + jnp.where(table[2 * n + 1, c] < cap, 0, E)
                turn[n * K + c : n * K + c + 1, 0:tok] = code.astype(f32)
        codes_f = jnp.transpose(turn[...])[0:tok].astype(jnp.int32)

    def normed_block(raw):
        wide = raw.astype(f32)
        inverse = lax.rsqrt(jnp.mean(wide * wide, axis=-1, keepdims=True) + norm_eps)
        scaled = wide * inverse
        return (scaled * gain[...]).astype(bf16), inverse

    lane = lax.broadcasted_iota(jnp.int32, (tok, E), 1)

    def gating(normed, first):
        logits = lax.dot_general(
            normed.astype(f32), router_t[...], NT, precision=highest, preferred_element_type=f32
        )
        probs = jax.nn.sigmoid(logits)
        picked = jnp.zeros((tok, E), f32)
        kept = jnp.zeros((tok, E), f32)
        for c in range(K):
            code = codes_f[:, first + c : first + c + 1]
            held = (code == lane).astype(f32)
            kept += held
            picked += held + (code == lane + E).astype(f32)
        total = jnp.sum(picked * probs, axis=-1, keepdims=True)
        return logits, probs, picked, kept, total, kept * (route_scale * probs / total)

    with jax.named_scope("p05_gating"):
        normed_a, _ = normed_block(X[0, k, j0])
        N[k, j0] = normed_a
        gates_a = gating(normed_a, 0)[5]
        normed_b, inverse_b = normed_block(X[1, k, j0])
        N2[k, j0] = normed_b
        logits_b, probs_b, picked_b, kept_b, total_b, gates_b = gating(normed_b, K)
        own[0, :, 0:E] = logits_b
        own[1, :, 0:E] = probs_b
        own[2, :, 0:E] = picked_b
        own[3, :, 0:E] = kept_b
        own[4, :, 0:E] = jnp.broadcast_to(total_b, (tok, E))
        own[5, :, 0:E] = jnp.broadcast_to(inverse_b, (tok, E))
        turn[...] = jnp.zeros((128, 128), f32)
        turn[0:tok, 0:E] = gates_a
        turn[0:tok, E : 2 * E] = gates_b
        mine = k * J + j0
        GT[mine] = jnp.transpose(turn[...])[0 : 2 * E]
        for d in range(1, n_e):
            piece(
                rcopy(GT.at[mine], GT.at[mine], sg.at[0], rg.at[0], {"expert": lax.rem(me + d, n_e)})
            )
        blocks = GT.at[pl.ds(0, n_e - 1)]
        all_gates = rcopy(blocks, blocks, sg.at[0], rg.at[0], {"expert": sib})
        started.append(all_gates)
        send_own(1)
        send_own(2)
        send_rest(1)
        send_rest(2)
        weights = [[], [], []]
        pairs = [(i, e) for e in range(per) for i in (0, 1)] + [(2, e) for e in range(per)]
        for i, e in pairs:
            weights[i].append(load(((wg_h, wu_h, wd_h)[i]).at[e], (wg, wu, wd)[i].at[e], w_sem.at[i, e]))

    to_tok = {}
    hops = [[(d, c) for d in range(1, J) for c in range(CH[s])] for s in range(3)]

    def relay_first(s, d, c):
        src = lax.rem(j0 - d + J, J)
        c1[s][d - 1][c].wait_recv()
        part = X.at[s, k, src, rows_of(s, c), lead(x)]
        for t in range(1, n_t):
            to_tok[s, d, c, t] = piece(
                rcopy(
                    part,
                    part,
                    stok.at[d - 1, t - 1],
                    rtok.at[d - 1, t - 1, first_slot[s] + c],
                    {"token": lax.rem(x + t, n_t)},
                )
            )
        piece(to_sib(s, d, c, part))

    def to_sib(s, d, c, part):
        return rcopy(
            part, part, ssib.at[d - 1], rsib.at[d - 1, first_slot[s] + c], {"expert": sib}
        )

    def relay_second(s, d, c):
        src = lax.rem(j0 - d + J, J)
        for t in range(1, n_t):
            to_tok[s, d, c, t].wait_recv()
            part = X.at[s, k, src, rows_of(s, c), lead(lax.rem(x - t + n_t, n_t))]
            piece(to_sib(s, d, c, part))

    def drain(ref, ss, rs):
        started.append(rcopy(ref, ref, ss, rs, {"expert": sib}))

    drain(X.at[:, k, j0], s0.at[0], r0.at[0])
    for d in range(1, J):
        src = lax.rem(j0 - d + J, J)
        drain(X.at[:, k, j0, :, pl.ds(0, W + Q)], s1.at[d - 1], r1.at[d - 1, 0])
        drain(X.at[:, k, src], ssib.at[d - 1], rsib.at[d - 1, 0])
        for t in range(1, n_t):
            drain(X.at[:, k, src, :, pl.ds(0, L)], stok.at[d - 1, t - 1], rtok.at[d - 1, t - 1, 0])
    drain(Pb.at[:, :, 1 - k], sR1.at[0], rR1.at[0, 0, 0])
    drain(QA, sR2A.at[0], rR2A.at[0, 0, 0])
    drain(ZA, sR3A.at[0], rR3A.at[0, 0, 0])
    drain(QB, sR2B.at[0], rR2B.at[0, 0, 0, 0])
    drain(ZB.at[:, pl.ds(1, n_t - 1)], sR3B.at[0], rR3B.at[0, 0, 0])

    def arrive(s, d, c):
        src = lax.rem(j0 - d + J, J)
        to_sib(s, d, c, X.at[s, 1 - k, src, rows_of(s, c), pl.ds(0, n_t * L)]).wait_recv()

    def relay_trail(s):
        for d in range(1, J if Q else 1):
            src = lax.rem(j0 - d + J, J)
            both = X.at[s, k, src, :, pl.ds(0, 2 * Q)]
            rcopy(both, both, s1.at[d - 1], r1t.at[d - 1, s], {"expert": sib}).wait_recv()
            for share in range(2):
                part = X.at[s, k, src, :, trail(share)]
                piece(rcopy(part, part, ssib.at[d - 1], rsibt.at[d - 1, s], {"expert": sib}))

    def arrive_trail(s):
        for d in range(1, J if Q else 1):
            src = lax.rem(j0 - d + J, J)
            both = X.at[s, 1 - k, src, :, pl.ds(0, 2 * Q)]
            rcopy(both, both, ssib.at[d - 1], rsibt.at[d - 1, s], {"expert": sib}).wait_recv()

    def normalize_rows(s, p, d, c):
        src = lax.rem(j0 - d + J, J)
        N[p, src, rows_of(s, c)] = normed_block(X[s, p, src, rows_of(s, c)])[0]

    M = T
    wide_lane = lax.broadcasted_iota(jnp.int32, (M, 128), 1)

    def column(s, e):
        want = s * E + me * per + e
        picked = jnp.where(wide_lane == want, G[...].reshape(M, 128), 0.0)
        return jnp.sum(picked, axis=1, keepdims=True)

    def put(ref, e, value):
        ref[e] = value.astype(bf16)

    def fwd_part(e):
        rows = N[...].reshape(M, D)
        gate = mm(rows, wg[e], NT)
        up = mm(rows, wu[e], NT)
        put(act, e, gate * jax.nn.sigmoid(gate) * up * column(0, e))

    def bwd_part(e):
        rows = N2[...].reshape(M, D)
        gate = mm(rows, wg[e], NT)
        up = mm(rows, wu[e], NT)
        grad_act = mm(X[2].reshape(M, D), wd[e], NT)
        sigma = jax.nn.sigmoid(gate)
        silu = gate * sigma
        ggv = grad_act * up * sigma * (1.0 + gate * (1.0 - sigma))
        guv = grad_act * silu
        col = column(1, e)
        dg = jnp.sum(guv * up, axis=1, keepdims=True)
        corr = col * jnp.sum(ggv * gate + guv * up, axis=1, keepdims=True)
        both = jnp.where(wide_lane == e, dg, 0.0) + jnp.where(wide_lane == per, corr, 0.0)
        Sc[...] = both if e == 0 else Sc[...] + both
        put(gg, e, ggv * col)
        put(gu, e, guv * col)

    def produce(r, h, ti, emit):
        at = pl.multiple_of(lax.rem(x + ti, n_t) * W + h * H, H)
        Pb[r, h, :, ti] = emit(at).astype(bf16).reshape(2, J, tok, H)
        return piece(
            rcopy(
                Pb.at[r, h, 1 - k, ti],
                R1.at[r, h, ti],
                sR1.at[0],
                rR1.at[r, h, ti],
                {"expert": sib},
            )
        )

    split = J == 2
    NP = 2 if split and H % 256 == 0 else 1
    HP = H // NP

    def sub(n):
        return slice(n * HP, (n + 1) * HP)

    def token_part(r, ti, j, n, slot):
        at = (r, ti - 1, j, slice(None), sub(n)) if split else (r, ti - 1)
        return piece(
            rcopy(
                QA.at[at],
                R2A.at[at],
                sR2A.at[0],
                rR2A.at[r, ti - 1, slot],
                {"token": lax.rem(x + ti, n_t)},
            )
        )

    def token_first(r, ti, copy):
        copy.wait_recv()
        QA[r, ti - 1] = (Pb[r, 0, k, ti].astype(f32) + R1[r, 0, ti].astype(f32)).astype(bf16)
        return [token_part(r, ti, 1 - j0, n, n) for n in range(NP)]

    def token_rest(r, sent):
        if split:
            for ti in range(1, n_t):
                sent[ti - 1] += [token_part(r, ti, j0, n, NP + n) for n in range(NP)]

    def expert_first(r, ti, copy):
        copy.wait_recv()
        sent = [[] for _ in range(NP)]
        for d in range(1, J):
            jd = lax.rem(j0 + d, J)
            total = Pb[r, 1, k, ti, jd].astype(f32) + R1[r, 1, ti, jd].astype(f32)
            QB[r, d - 1, ti] = total.astype(bf16)
            for n in range(NP):
                at = (r, d - 1, ti, slice(None), sub(n))
                sent[n].append(
                    piece(
                        rcopy(
                            QB.at[at],
                            R2B.at[at],
                            sR2B.at[0],
                            rR2B.at[r, d - 1, ti, n],
                            {"expert": jd * 2 + k},
                        )
                    )
                )
        return sent

    def first_total(r, j, n):
        total = Pb[r, 0, k, 0, j, :, sub(n)].astype(f32) + R1[r, 0, 0, j, :, sub(n)].astype(f32)
        for ti in range(1, n_t):
            total += R2A[r, ti - 1, j, :, sub(n)].astype(f32)
        return total

    def then_expert(r, first, sent):
        first.wait_recv()
        out = []
        for n in range(NP):
            for c in sent:
                c[n].wait_recv()
            out.append([])
            for d in range(1, J):
                jd = lax.rem(j0 + d, J)
                at = (r, d - 1, slice(None), sub(n))
                ZA[at] = first_total(r, jd, n).astype(bf16)
                out[n].append(
                    piece(
                        rcopy(
                            ZA.at[at],
                            R3A.at[at],
                            sR3A.at[0],
                            rR3A.at[r, d - 1, n],
                            {"expert": jd * 2 + k},
                        )
                    )
                )
        return out

    def own_token(r, ti, n, sent):
        for c in sent[n]:
            c.wait_recv()
        total = Pb[r, 1, k, ti, j0, :, sub(n)].astype(f32) + R1[r, 1, ti, j0, :, sub(n)].astype(f32)
        for d in range(1, J):
            total += R2B[r, d - 1, ti, :, sub(n)].astype(f32)
        return total

    def then_token(r, ti, sent):
        out = []
        for n in range(NP):
            at = (r, ti, slice(None), sub(n))
            ZB[at] = own_token(r, ti, n, sent).astype(bf16)
            to = (r, ti - 1, slice(None), sub(n))
            out.append(
                piece(
                    rcopy(
                        ZB.at[at],
                        R3B.at[to],
                        sR3B.at[0],
                        rR3B.at[r, ti - 1, n],
                        {"token": lax.rem(x + ti, n_t)},
                    )
                )
            )
        return out

    def last_a(r, n, mine, sent):
        if split:
            for c in mine:
                c[NP + n].wait_recv()
        total = first_total(r, j0, n)
        for c in sent[n]:
            c.wait_recv()
        for d in range(1, J):
            total += R3A[r, d - 1, :, sub(n)].astype(f32)
        return total

    def last_b(r, n, mine, sent):
        total = own_token(r, 0, n, mine)
        for c in sent:
            c[n].wait_recv()
        for ti in range(1, n_t):
            total += R3B[r, ti - 1, :, sub(n)].astype(f32)
        return total

    pieces = [(h, n) for h in range(2) for n in range(NP)]

    def piece_cols(h, n):
        return pl.ds(pl.multiple_of(x * W + h * H + n * HP, 128), HP)

    def send_next(h, n):
        part = (0, slice(None), pl.ds(h * H + n * HP, HP))
        return rcopy(
            zbuf.at[part],
            out_next.at[part],
            sz.at[0, h, n],
            rz.at[0, h, n],
            {"segment": lax.rem(seg + 1, n_seg)},
        )

    def send_prev(h, n):
        part = (slice(None), pl.ds(h * H + n * HP, HP))
        return rcopy(
            zbuf.at[(1,) + part],
            out_prev.at[(0,) + part],
            sz.at[1, h, n],
            rz.at[1, h, n],
            {"segment": lax.rem(seg - 1 + n_seg, n_seg)},
        )

    def emit_fwd(at):
        total = None
        for e in range(per):
            piece = mm(act[e], wd[e, :, pl.ds(at, H)])
            total = piece if total is None else total + piece
        return total

    def emit_bwd(at):
        total = None
        for e in range(per):
            for grads, w in ((gg, wg), (gu, wu)):
                piece = mm(grads[e], w[e, :, pl.ds(at, H)])
                total = piece if total is None else total + piece
        return total

    def finish_next(h, n, mixed):
        rows = X[0, k, j0, :, piece_cols(h, n)].astype(f32) + mixed
        zbuf[0, :, pl.ds(h * H + n * HP, HP)] = rows.astype(bf16)

        @pl.when(seg < n_seg - 1)
        def _():
            send_next(h, n).start()

    order = [*range(1, n_t), 0]

    def produce_all(r, emit, tag):
        pa = [None] * n_t
        pb = [None] * n_t
        qa = []
        qb = [None] * n_t
        for ti in range(1, n_t):
            with jax.named_scope(f"{tag}_a{ti}"):
                pa[ti] = produce(r, 0, ti, emit)
            with jax.named_scope(f"{tag}_b{ti}"):
                pb[ti] = produce(r, 1, ti, emit)
                qa.append(token_first(r, ti, pa[ti]))
        with jax.named_scope(f"{tag}_a0"):
            pa[0] = produce(r, 0, 0, emit)
            for ti in range(1, n_t):
                qb[ti] = expert_first(r, ti, pb[ti])
            token_rest(r, qa)
        with jax.named_scope(f"{tag}_b0"):
            pb[0] = produce(r, 1, 0, emit)
        return pa[0], pb[0], qa, qb

    with jax.named_scope("p07_norm"):
        c0[0].wait_recv()
        N[1 - k, j0] = normed_block(X[0, 1 - k, j0])[0]
    with jax.named_scope("p08_relay1"):
        for d, c in hops[0]:
            relay_first(0, d, c)
        relay_trail(0)
    with jax.named_scope("p09_relay2"):
        for d, c in hops[0]:
            relay_second(0, d, c)
            normalize_rows(0, k, d, c)
    with jax.named_scope("p10_arrive"):
        first_b = [h for h in hops[1] if h[1] == 0]
        later_b = [h for h in hops[1] if h[1] > 0]
        for d, c in first_b:
            relay_first(1, d, c)
        c0[1].wait_recv()
        N2[1 - k, j0] = normed_block(X[1, 1 - k, j0])[0]
        all_gates.wait_recv()
        turn[...] = jnp.zeros((128, 128), f32)
        for p in range(2):
            for j in range(J):
                turn[0 : 2 * E] = GT[p * J + j]
                G[p, j] = jnp.transpose(turn[...])[0:tok]
        arrive_trail(0)
        for d, c in hops[0]:
            arrive(0, d, c)
            normalize_rows(0, 1 - k, d, c)

    with jax.named_scope("p11_fwd0"):
        weights[0][0].wait()
        weights[1][0].wait()
        fwd_part(0)
    with jax.named_scope("p12_relay"):
        for d, c in later_b:
            relay_first(1, d, c)
        for d, c in hops[2]:
            relay_first(2, d, c)
    with jax.named_scope("p13_fwd1"):
        for e in range(1, per):
            weights[0][e].wait()
            weights[1][e].wait()
            fwd_part(e)
        for e in range(per):
            weights[2][e].wait()
    with jax.named_scope("p13b_relay"):
        for d, c in first_b:
            relay_second(1, d, c)
        relay_trail(1)
        relay_trail(2)
    with jax.named_scope("p14_prod"):
        pa = []
        pb = []
        for ti in order[:-1]:
            pa.append(produce(0, 0, ti, emit_fwd))
            pb.append(produce(0, 1, ti, emit_fwd))
        for d, c in later_b:
            relay_second(1, d, c)
        pa.append(produce(0, 0, 0, emit_fwd))
        pb.append(produce(0, 1, 0, emit_fwd))
    with jax.named_scope("p14z_relay"):
        for d, c in hops[2]:
            relay_second(2, d, c)
        arrive_trail(1)
        for d, c in hops[1]:
            arrive(1, d, c)
        for d in range(1, J):
            src = lax.rem(j0 - d + J, J)
            for p in range(2):
                N2[p, src] = normed_block(X[1, p, src])[0]
    with jax.named_scope("p16_first"):
        qa = [token_first(0, ti, pa[n]) for n, ti in enumerate(order[:-1])]
        qb = [None] * n_t
        for n, ti in enumerate(order[:-1]):
            qb[ti] = expert_first(0, ti, pb[n])
        token_rest(0, qa)
    with jax.named_scope("p16b_cot"):
        c0[2].wait_recv()
        arrive_trail(2)
        for d, c in hops[2]:
            arrive(2, d, c)
    with jax.named_scope("p17_bwd"):
        for e in range(per):
            bwd_part(e)
    with jax.named_scope("p18_fsec"):
        za = then_expert(0, pa[-1], qa)
        zb = [then_token(0, ti, qb[ti]) for ti in range(1, n_t)]
        qb[0] = expert_first(0, 0, pb[-1])

    with jax.named_scope("p19_sendS"):
        flipped = jnp.transpose(Sc[...])[0:8]
        for p in range(2):
            for j in range(J):
                at = (p * J + j) * tok
                Sb[j * 2 + p] = flipped[:, at : at + tok]
        for de in range(n_e):
            for dt in range(n_t):
                if de or dt:
                    to = lax.rem(me + de, n_e)
                    piece(
                        rcopy(
                            Sb.at[to],
                            RS.at[me * n_t + x],
                            sS.at[0],
                            rS.at[0],
                            {"expert": to, "token": lax.rem(x + dt, n_t)},
                        )
                    )
        blocks = RS.at[pl.ds(0, n_e * n_t - 1)]
        all_sums = rcopy(blocks, blocks, sS.at[0], rS.at[0], {"expert": sib})
        started.append(all_sums)
        RS[me * n_t + x] = Sb[me]

    qa0, zb0 = qa, zb
    pa, pb, qa, qc = produce_all(1, emit_bwd, "p20_prod")
    with jax.named_scope("p21_first"):
        zc = then_expert(1, pa, qa)
    with jax.named_scope("p23_dgt"):
        all_sums.wait_recv()
        DGT[...] = jnp.zeros(DGT.shape, f32)
        corr = jnp.zeros((1, tok), f32)
        for e in range(n_e):
            total = RS[e * n_t]
            for t in range(1, n_t):
                total += RS[e * n_t + t]
            DGT[e * per : (e + 1) * per, 0:tok] = total[0:per]
            corr += total[per : per + 1]
        DGT[E : E + 1, 0:tok] = corr
        turned = jnp.transpose(DGT[...])[0:tok]
        logits_b = own[0, :, 0:E]
        probs_b = own[1, :, 0:E]
        total_b = own[4, :, 0:E]
        inverse_b = own[5, :, 0:1]
        dgates = jnp.where(own[3, :, 0:E] > 0.5, turned[:, 0:E], 0.0)
        spread = jnp.sum(dgates * probs_b, axis=-1, keepdims=True)
        dprobs = route_scale * dgates / total_b - route_scale * spread / (total_b * total_b)
        dlogits = jnp.where(own[2, :, 0:E] > 0.5, dprobs * probs_b * (1.0 - probs_b), 0.0)
        mean_all = (turned[:, E : E + 1] + jnp.sum(dlogits * logits_b, axis=-1, keepdims=True)) / D
        router_own = lax.dot_general(
            dlogits, router_t[:, cols(x)], NN, precision=highest, preferred_element_type=f32
        )
        gain_own = gain[:, cols(x)]
        scaled_own = X[1, k, j0, :, cols(x)].astype(f32) * inverse_b
        cot_own = X[2, k, j0, :, cols(x)].astype(f32)
        base = cot_own + inverse_b * (router_own * gain_own - scaled_own * mean_all)
        scale_own = inverse_b * gain_own
        own_base[0] = base
        own_base[1] = scale_own
        qc[0] = expert_first(1, 0, pb)

    with jax.named_scope("p24_second"):
        zb = [then_token(1, ti, qc[ti]) for ti in range(1, n_t)]

    with jax.named_scope("p22_finnext"):
        for n in range(NP):
            finish_next(0, n, last_a(0, n, qa0, za))
        for n in range(NP):
            finish_next(1, n, last_b(0, n, qb[0], zb0))

        @pl.when(seg == 0)
        def _():
            out_next[...] = jnp.zeros(out_next.shape, bf16)

        @pl.when(seg == n_seg - 1)
        def _():
            out_prev[...] = jnp.zeros(out_prev.shape, bf16)

    def finish_prev(h, n, mixed):
        at = slice(h * H + n * HP, h * H + (n + 1) * HP)
        zbuf[1, :, at] = (own_base[0, :, at] + own_base[1, :, at] * mixed).astype(bf16)

        @pl.when(seg > 0)
        def _():
            send_prev(h, n).start()

    with jax.named_scope("p25_lasta"):
        for n in range(NP):
            finish_prev(0, n, last_a(1, n, qa, zc))
    with jax.named_scope("p26_lastb"):
        for n in range(NP):
            finish_prev(1, n, last_b(1, n, qc[0], zb))

    with jax.named_scope("p27_end"):
        for c in started:
            c.wait_send()

        @pl.when(seg < n_seg - 1)
        def _():
            for h, n in pieces:
                send_next(h, n).wait_send()
                send_prev(h, n).wait_recv()

        @pl.when(seg > 0)
        def _():
            for h, n in pieces:
                send_prev(h, n).wait_send()
                send_next(h, n).wait_recv()


def settle(next_in, prev_in, next_out, prev_out):
    next_out[...] = next_in[...]
    prev_out[...] = prev_in[...]


def body(
    fwd_acts,
    fwd_ids,
    fwd_slots,
    bwd_acts,
    bwd_ids,
    bwd_slots,
    bwd_grad,
    norm_gain,
    router,
    w_gate,
    w_up,
    w_down,
):
    E = router.shape[2]
    per, D, F = w_gate.shape
    n_seg = lax.axis_size("segment")
    n_e = lax.axis_size("expert")
    n_t = lax.axis_size("token")
    tok = fwd_acts.shape[1]
    K = fwd_ids.shape[2]
    cap = max(2, min(3 * tok * K // (4 * E), tok - 1))
    W = D // n_t
    J = n_e // 2
    T = n_e * tok
    V = pltpu.VMEM
    dma = pltpu.SemaphoreType.DMA
    peers = max(J - 1, 1)
    CH = tuple(max(n // peers, 1) for n in (4, 2, 1))
    toks = max(n_t - 1, 1)
    scratch = [
        V((3, 2, J, tok, D), bf16),
        V((2, J, tok, D), bf16),
        V((2, J, tok, D), bf16),
        V((2, J, tok, 128), f32),
        V((n_e, 2 * E, 128), f32),
        V((per, F, D), bf16),
        V((per, F, D), bf16),
        V((per, F, D), bf16),
        V((per, T, F), bf16),
        V((per, T, F), bf16),
        V((per, T, F), bf16),
        V((2, 2, 2, n_t, J, tok, W // 2), bf16),
        V((2, 2, n_t, J, tok, W // 2), bf16),
        V((2, toks, J, tok, W // 2), bf16),
        V((2, toks, J, tok, W // 2), bf16),
        V((2, peers, tok, W // 2), bf16),
        V((2, peers, tok, W // 2), bf16),
        V((2, peers, n_t, tok, W // 2), bf16),
        V((2, peers, n_t, tok, W // 2), bf16),
        V((2, n_t, tok, W // 2), bf16),
        V((2, toks, tok, W // 2), bf16),
        V((T, 128), f32),
        V((n_e, 8, tok), f32),
        V((n_e * n_t, 8, tok), f32),
        V((128, 128), f32),
        V((6, tok, 128), f32),
        V((2, tok, W), f32),
        V((2, tok, W), bf16),
        V((128, 128), f32),
        V((4, K, 1, tok), jnp.int32),
        V((1, D), f32),
        V((E, D), f32),
        dma((3, per)),
        dma((1,)),
        dma((3,)),
        dma((1,)),
        dma((3,)),
        dma((peers,)),
        dma((peers, sum(CH))),
        dma((peers, 3)),
        dma((1,)),
        dma((1,)),
        dma((peers,)),
        dma((peers, sum(CH))),
        dma((peers, 3)),
        dma((peers, toks)),
        dma((peers, toks, sum(CH))),
        dma((1,)),
        dma((2, 2, n_t)),
        dma((1,)),
        dma((2, toks, 4)),
        dma((1,)),
        dma((2, peers, 2)),
        dma((1,)),
        dma((2, peers, n_t, 2)),
        dma((1,)),
        dma((2, toks, 2)),
        dma((1,)),
        dma((1,)),
        dma((2, 2, 2)),
        dma((2, 2, 2)),
    ]
    held = sum(
        int(np.prod(s.shape)) * jnp.dtype(s.dtype).itemsize
        for s in scratch
        if s.memory_space == V
    )
    vm = pl.BlockSpec(memory_space=pltpu.VMEM)
    hbm = pl.BlockSpec(memory_space=pltpu.HBM)
    out = jax.ShapeDtypeStruct((1, tok, W), bf16)
    sizes = (n_seg, n_e, n_t, per, E, tok, D, F, K, CH, cap)
    moved = pl.pallas_call(
        functools.partial(kernel, sizes),
        out_shape=(out, out),
        in_specs=[hbm] * 12,
        out_specs=(vm, vm),
        scratch_shapes=scratch,
        compiler_params=pltpu.CompilerParams(
            collective_id=0, has_side_effects=True, vmem_limit_bytes=held + 9 * 1024 * 1024
        ),
        name="relay_moe",
    )(
        *(
            pltpu.with_memory_space_constraint(t, pltpu.HBM)
            for t in (
                fwd_acts,
                bwd_acts,
                bwd_grad,
                *(jnp.transpose(t, (2, 0, 1)) for t in (fwd_ids, fwd_slots, bwd_ids, bwd_slots)),
                norm_gain,
                router[0].T,
                jnp.swapaxes(w_gate, 1, 2),
                jnp.swapaxes(w_up, 1, 2),
                w_down,
            )
        )
    )
    return pl.pallas_call(
        settle, out_shape=(out, out), in_specs=[vm] * 2, out_specs=(vm, vm), name="settle",
        compiler_params=pltpu.CompilerParams(vmem_limit_bytes=2 * 1024 * 1024),
    )(*moved)


def solution(mesh):
    return jax.shard_map(
        body,
        mesh=mesh,
        in_specs=(
            P("segment", "expert", None),
            P("segment", "expert", None),
            P("segment", "expert", None),
            P("segment", "expert", None),
            P("segment", "expert", None),
            P("segment", "expert", None),
            P("segment", "expert", None),
            P("segment", None),
            P("segment", None, None),
            P("expert", None, "token"),
            P("expert", None, "token"),
            P("expert", "token", None),
        ),
        out_specs=(P("segment", "expert", "token"), P("segment", "expert", "token")),
        check_vma=False,
    )
```

```python
import functools

import jax
import jax.numpy as jnp
import numpy as np
from jax import lax
from jax.experimental import pallas as pl
from jax.experimental.pallas import tpu as pltpu
from jax.sharding import PartitionSpec as P

route_scale = 2.446
norm_eps = 1e-06
highest = lax.Precision.HIGHEST
MESH = pl.DeviceIdType.MESH
f32 = jnp.float32
bf16 = jnp.bfloat16
NT = (((1,), (1,)), ((), ()))
NN = (((1,), (0,)), ((), ()))


def mm(a, b, dims=NN):
    return lax.dot_general(a, b, dims, preferred_element_type=f32)


def kernel(
    sizes,
    fa,
    ba,
    bg,
    ids_a,
    slots_a,
    ids_b,
    slots_b,
    gain_h,
    router_h,
    wg_h,
    wu_h,
    wd_h,
    out_next,
    out_prev,
    X,
    N,
    N2,
    G,
    GT,
    wg,
    wu,
    wd,
    act,
    gg,
    gu,
    Pb,
    R1,
    QA,
    R2A,
    ZA,
    R3A,
    QB,
    R2B,
    ZB,
    R3B,
    Sc,
    Sb,
    RS,
    DGT,
    own,
    own_base,
    zbuf,
    turn,
    table,
    gain,
    router_t,
    w_sem,
    l_sem,
    i_sem,
    s0,
    r0,
    s1,
    r1,
    r1t,
    sg,
    rg,
    ssib,
    rsib,
    rsibt,
    stok,
    rtok,
    sR1,
    rR1,
    sR2A,
    rR2A,
    sR3A,
    rR3A,
    sR2B,
    rR2B,
    sR3B,
    rR3B,
    sS,
    rS,
    sz,
    rz,
):
    n_seg, n_e, n_t, per, E, tok, D, F, K, CH, cap = sizes
    J = n_e // 2
    W = D // n_t
    H = W // 2
    T = n_e * tok
    seg = lax.axis_index("segment")
    me = lax.axis_index("expert")
    x = lax.axis_index("token")
    k = lax.rem(me, 2)
    j0 = me // 2
    sib = j0 * 2 + 1 - k

    def cols(share):
        return pl.ds(pl.multiple_of(share * W, 128), W)

    Q = W // 4 if n_t == 2 and W % 512 == 0 else 0
    L = W - Q

    def lead(share):
        return pl.ds(pl.multiple_of(share * W, 128), L)

    def trail(share):
        return pl.ds(pl.multiple_of(share * W + L, 128), Q)

    first_slot = [sum(CH[:s]) for s in range(4)]

    def rows_of(s, c):
        R = tok // CH[s]
        return slice(c * R, (c + 1) * R)

    def rcopy(src, dst, ss, rs, dev):
        return pltpu.make_async_remote_copy(
            src_ref=src, dst_ref=dst, send_sem=ss, recv_sem=rs, device_id=dev, device_id_type=MESH
        )

    started = []

    def go(copy):
        copy.start()
        started.append(copy)
        return copy

    def piece(copy):
        copy.start()
        return copy

    def load(src, dst, sem):
        c = pltpu.make_async_copy(src, dst, sem)
        c.start()
        return c

    with jax.named_scope("p01_local"):
        ins = (fa, ba, bg)
        local = [load(ins[s].at[0], X.at[s, k, j0], l_sem.at[min(s, 1)]) for s in range(3)]
        rest = X.at[pl.ds(1, 2), k, j0]
        local = [local[0], pltpu.make_async_copy(rest, rest, l_sem.at[1])]
        small = [load(ref, table.at[n], i_sem.at[0]) for n, ref in enumerate((ids_a, slots_a, ids_b, slots_b))]
        small = [pltpu.make_async_copy(table, table, i_sem.at[0])]
        small.append(load(gain_h, gain, i_sem.at[1]))
        small.append(load(router_h, router_t, i_sem.at[2]))

        barrier = pltpu.get_barrier_semaphore()
        for de in range(n_e):
            for dt in range(n_t):
                if de or dt:
                    pl.semaphore_signal(
                        barrier,
                        inc=1,
                        device_id={"expert": lax.rem(me + de, n_e), "token": lax.rem(x + dt, n_t)},
                        device_id_type=MESH,
                    )

        @pl.when(seg > 0)
        def _():
            pl.semaphore_signal(barrier, inc=1, device_id={"segment": seg - 1}, device_id_type=MESH)

        @pl.when(seg < n_seg - 1)
        def _():
            pl.semaphore_signal(barrier, inc=1, device_id={"segment": seg + 1}, device_id_type=MESH)

    local[0].wait()
    with jax.named_scope("p02_barrier"):
        inner = jnp.where(seg > 0, 1, 0) + jnp.where(seg < n_seg - 1, 1, 0)
        pl.semaphore_wait(barrier, n_e * n_t - 1 + inner)

    c0 = [None] * 3
    c1 = [None] * 3

    def send_own(s):
        c1[s] = [
            [
                piece(
                    rcopy(
                        X.at[s, k, j0, rows_of(s, c), lead(x)],
                        X.at[s, k, j0, rows_of(s, c), lead(x)],
                        s1.at[d - 1],
                        r1.at[d - 1, first_slot[s] + c],
                        {"expert": lax.rem(j0 + d, J) * 2 + k},
                    )
                )
                for c in range(CH[s])
            ]
            for d in range(1, J)
        ]

    def send_rest(s):
        for d in range(1, J):
            for share in range(2 if Q else 0):
                part = X.at[s, k, j0, :, trail(share)]
                to = {"expert": lax.rem(j0 + d, J) * 2 + k}
                piece(rcopy(part, part, s1.at[d - 1], r1t.at[d - 1, s], to))
        c0[s] = piece(rcopy(X.at[s, k, j0], X.at[s, k, j0], s0.at[0], r0.at[s], {"expert": sib}))

    with jax.named_scope("p03_send"):
        send_own(0)
        send_rest(0)
    with jax.named_scope("p04_codes"):
        for c in small:
            c.wait()
        turn[...] = jnp.zeros((128, 128), f32)
        for n in range(2):
            for c in range(K):
                code = table[2 * n, c] + jnp.where(table[2 * n + 1, c] < cap, 0, E)
                turn[n * K + c : n * K + c + 1, 0:tok] = code.astype(f32)
        codes_f = jnp.transpose(turn[...])[0:tok].astype(jnp.int32)

    def normed_block(raw):
        wide = raw.astype(f32)
        inverse = lax.rsqrt(jnp.mean(wide * wide, axis=-1, keepdims=True) + norm_eps)
        scaled = wide * inverse
        return (scaled * gain[...]).astype(bf16), inverse

    lane = lax.broadcasted_iota(jnp.int32, (tok, E), 1)

    def gating(normed, first):
        logits = lax.dot_general(
            normed.astype(f32), router_t[...], NT, precision=highest, preferred_element_type=f32
        )
        probs = jax.nn.sigmoid(logits)
        picked = jnp.zeros((tok, E), f32)
        kept = jnp.zeros((tok, E), f32)
        for c in range(K):
            code = codes_f[:, first + c : first + c + 1]
            held = (code == lane).astype(f32)
            kept += held
            picked += held + (code == lane + E).astype(f32)
        total = jnp.sum(picked * probs, axis=-1, keepdims=True)
        return logits, probs, picked, kept, total, kept * (route_scale * probs / total)

    with jax.named_scope("p05_gating"):
        local[1].wait()
        normed_a, _ = normed_block(X[0, k, j0])
        N[k, j0] = normed_a
        gates_a = gating(normed_a, 0)[5]
        normed_b, inverse_b = normed_block(X[1, k, j0])
        N2[k, j0] = normed_b
        logits_b, probs_b, picked_b, kept_b, total_b, gates_b = gating(normed_b, K)
        own[0, :, 0:E] = logits_b
        own[1, :, 0:E] = probs_b
        own[2, :, 0:E] = picked_b
        own[3, :, 0:E] = kept_b
        own[4, :, 0:E] = jnp.broadcast_to(total_b, (tok, E))
        own[5, :, 0:E] = jnp.broadcast_to(inverse_b, (tok, E))
        turn[...] = jnp.zeros((128, 128), f32)
        turn[0:tok, 0:E] = gates_a
        turn[0:tok, E : 2 * E] = gates_b
        mine = k * J + j0
        GT[mine] = jnp.transpose(turn[...])[0 : 2 * E]
        for d in range(1, n_e):
            piece(
                rcopy(GT.at[mine], GT.at[mine], sg.at[0], rg.at[0], {"expert": lax.rem(me + d, n_e)})
            )
        blocks = GT.at[pl.ds(0, n_e - 1)]
        all_gates = rcopy(blocks, blocks, sg.at[0], rg.at[0], {"expert": sib})
        started.append(all_gates)
        send_own(1)
        send_own(2)
        send_rest(1)
        send_rest(2)
        weights = [[], [], []]
        pairs = [(i, e) for e in range(per) for i in (0, 1)] + [(2, e) for e in range(per)]
        for i, e in pairs:
            weights[i].append(load(((wg_h, wu_h, wd_h)[i]).at[e], (wg, wu, wd)[i].at[e], w_sem.at[i, e]))

    to_tok = {}
    hops = [[(d, c) for d in range(1, J) for c in range(CH[s])] for s in range(3)]

    def relay_first(s, d, c):
        src = lax.rem(j0 - d + J, J)
        c1[s][d - 1][c].wait_recv()
        part = X.at[s, k, src, rows_of(s, c), lead(x)]
        for t in range(1, n_t):
            to_tok[s, d, c, t] = piece(
                rcopy(
                    part,
                    part,
                    stok.at[d - 1, t - 1],
                    rtok.at[d - 1, t - 1, first_slot[s] + c],
                    {"token": lax.rem(x + t, n_t)},
                )
            )
        piece(to_sib(s, d, c, part))

    def to_sib(s, d, c, part):
        return rcopy(
            part, part, ssib.at[d - 1], rsib.at[d - 1, first_slot[s] + c], {"expert": sib}
        )

    def relay_second(s, d, c):
        src = lax.rem(j0 - d + J, J)
        for t in range(1, n_t):
            to_tok[s, d, c, t].wait_recv()
            part = X.at[s, k, src, rows_of(s, c), lead(lax.rem(x - t + n_t, n_t))]
            piece(to_sib(s, d, c, part))

    def drain(ref, ss, rs):
        started.append(rcopy(ref, ref, ss, rs, {"expert": sib}))

    drain(X.at[:, k, j0], s0.at[0], r0.at[0])
    for d in range(1, J):
        src = lax.rem(j0 - d + J, J)
        drain(X.at[:, k, j0, :, pl.ds(0, W + Q)], s1.at[d - 1], r1.at[d - 1, 0])
        drain(X.at[:, k, src], ssib.at[d - 1], rsib.at[d - 1, 0])
        for t in range(1, n_t):
            drain(X.at[:, k, src, :, pl.ds(0, L)], stok.at[d - 1, t - 1], rtok.at[d - 1, t - 1, 0])
    drain(Pb.at[:, :, 1 - k], sR1.at[0], rR1.at[0, 0, 0])
    drain(QA, sR2A.at[0], rR2A.at[0, 0, 0])
    drain(ZA, sR3A.at[0], rR3A.at[0, 0, 0])
    drain(QB, sR2B.at[0], rR2B.at[0, 0, 0, 0])
    drain(ZB.at[:, pl.ds(1, n_t - 1)], sR3B.at[0], rR3B.at[0, 0, 0])

    def arrive(s, d, c):
        src = lax.rem(j0 - d + J, J)
        to_sib(s, d, c, X.at[s, 1 - k, src, rows_of(s, c), pl.ds(0, n_t * L)]).wait_recv()

    def relay_trail(s):
        for d in range(1, J if Q else 1):
            src = lax.rem(j0 - d + J, J)
            both = X.at[s, k, src, :, pl.ds(0, 2 * Q)]
            rcopy(both, both, s1.at[d - 1], r1t.at[d - 1, s], {"expert": sib}).wait_recv()
            for share in range(2):
                part = X.at[s, k, src, :, trail(share)]
                piece(rcopy(part, part, ssib.at[d - 1], rsibt.at[d - 1, s], {"expert": sib}))

    def arrive_trail(s):
        for d in range(1, J if Q else 1):
            src = lax.rem(j0 - d + J, J)
            both = X.at[s, 1 - k, src, :, pl.ds(0, 2 * Q)]
            rcopy(both, both, ssib.at[d - 1], rsibt.at[d - 1, s], {"expert": sib}).wait_recv()

    def normalize_rows(s, p, d, c):
        src = lax.rem(j0 - d + J, J)
        N[p, src, rows_of(s, c)] = normed_block(X[s, p, src, rows_of(s, c)])[0]

    M = T
    wide_lane = lax.broadcasted_iota(jnp.int32, (M, 128), 1)

    def column(s, e):
        want = s * E + me * per + e
        picked = jnp.where(wide_lane == want, G[...].reshape(M, 128), 0.0)
        return jnp.sum(picked, axis=1, keepdims=True)

    def put(ref, e, value):
        ref[e] = value.astype(bf16)

    def fwd_part(e):
        rows = N[...].reshape(M, D)
        gate = mm(rows, wg[e], NT)
        up = mm(rows, wu[e], NT)
        put(act, e, gate * jax.nn.sigmoid(gate) * up * column(0, e))

    def bwd_part(e):
        rows = N2[...].reshape(M, D)
        gate = mm(rows, wg[e], NT)
        up = mm(rows, wu[e], NT)
        grad_act = mm(X[2].reshape(M, D), wd[e], NT)
        sigma = jax.nn.sigmoid(gate)
        silu = gate * sigma
        ggv = grad_act * up * sigma * (1.0 + gate * (1.0 - sigma))
        guv = grad_act * silu
        col = column(1, e)
        dg = jnp.sum(guv * up, axis=1, keepdims=True)
        corr = col * jnp.sum(ggv * gate + guv * up, axis=1, keepdims=True)
        both = jnp.where(wide_lane == e, dg, 0.0) + jnp.where(wide_lane == per, corr, 0.0)
        Sc[...] = both if e == 0 else Sc[...] + both
        put(gg, e, ggv * col)
        put(gu, e, guv * col)

    def produce(r, h, ti, emit):
        at = pl.multiple_of(lax.rem(x + ti, n_t) * W + h * H, H)
        Pb[r, h, :, ti] = emit(at).astype(bf16).reshape(2, J, tok, H)
        return piece(
            rcopy(
                Pb.at[r, h, 1 - k, ti],
                R1.at[r, h, ti],
                sR1.at[0],
                rR1.at[r, h, ti],
                {"expert": sib},
            )
        )

    split = J == 2
    NP = 2 if split and H % 256 == 0 else 1
    HP = H // NP

    def sub(n):
        return slice(n * HP, (n + 1) * HP)

    def token_part(r, ti, j, n, slot):
        at = (r, ti - 1, j, slice(None), sub(n)) if split else (r, ti - 1)
        return piece(
            rcopy(
                QA.at[at],
                R2A.at[at],
                sR2A.at[0],
                rR2A.at[r, ti - 1, slot],
                {"token": lax.rem(x + ti, n_t)},
            )
        )

    def token_first(r, ti, copy):
        copy.wait_recv()
        QA[r, ti - 1] = (Pb[r, 0, k, ti].astype(f32) + R1[r, 0, ti].astype(f32)).astype(bf16)
        return [token_part(r, ti, 1 - j0, n, n) for n in range(NP)]

    def token_rest(r, sent):
        if split:
            for ti in range(1, n_t):
                sent[ti - 1] += [token_part(r, ti, j0, n, NP + n) for n in range(NP)]

    def expert_first(r, ti, copy):
        copy.wait_recv()
        sent = [[] for _ in range(NP)]
        for d in range(1, J):
            jd = lax.rem(j0 + d, J)
            total = Pb[r, 1, k, ti, jd].astype(f32) + R1[r, 1, ti, jd].astype(f32)
            QB[r, d - 1, ti] = total.astype(bf16)
            for n in range(NP):
                at = (r, d - 1, ti, slice(None), sub(n))
                sent[n].append(
                    piece(
                        rcopy(
                            QB.at[at],
                            R2B.at[at],
                            sR2B.at[0],
                            rR2B.at[r, d - 1, ti, n],
                            {"expert": jd * 2 + k},
                        )
                    )
                )
        return sent

    def first_total(r, j, n):
        total = Pb[r, 0, k, 0, j, :, sub(n)].astype(f32) + R1[r, 0, 0, j, :, sub(n)].astype(f32)
        for ti in range(1, n_t):
            total += R2A[r, ti - 1, j, :, sub(n)].astype(f32)
        return total

    def then_expert(r, first, sent):
        first.wait_recv()
        out = []
        for n in range(NP):
            for c in sent:
                c[n].wait_recv()
            out.append([])
            for d in range(1, J):
                jd = lax.rem(j0 + d, J)
                at = (r, d - 1, slice(None), sub(n))
                ZA[at] = first_total(r, jd, n).astype(bf16)
                out[n].append(
                    piece(
                        rcopy(
                            ZA.at[at],
                            R3A.at[at],
                            sR3A.at[0],
                            rR3A.at[r, d - 1, n],
                            {"expert": jd * 2 + k},
                        )
                    )
                )
        return out

    def own_token(r, ti, n, sent):
        for c in sent[n]:
            c.wait_recv()
        total = Pb[r, 1, k, ti, j0, :, sub(n)].astype(f32) + R1[r, 1, ti, j0, :, sub(n)].astype(f32)
        for d in range(1, J):
            total += R2B[r, d - 1, ti, :, sub(n)].astype(f32)
        return total

    def then_token(r, ti, sent):
        out = []
        for n in range(NP):
            at = (r, ti, slice(None), sub(n))
            ZB[at] = own_token(r, ti, n, sent).astype(bf16)
            to = (r, ti - 1, slice(None), sub(n))
            out.append(
                piece(
                    rcopy(
                        ZB.at[at],
                        R3B.at[to],
                        sR3B.at[0],
                        rR3B.at[r, ti - 1, n],
                        {"token": lax.rem(x + ti, n_t)},
                    )
                )
            )
        return out

    def last_a(r, n, mine, sent):
        if split:
            for c in mine:
                c[NP + n].wait_recv()
        total = first_total(r, j0, n)
        for c in sent[n]:
            c.wait_recv()
        for d in range(1, J):
            total += R3A[r, d - 1, :, sub(n)].astype(f32)
        return total

    def last_b(r, n, mine, sent):
        total = own_token(r, 0, n, mine)
        for c in sent:
            c[n].wait_recv()
        for ti in range(1, n_t):
            total += R3B[r, ti - 1, :, sub(n)].astype(f32)
        return total

    pieces = [(h, n) for h in range(2) for n in range(NP)]

    def piece_cols(h, n):
        return pl.ds(pl.multiple_of(x * W + h * H + n * HP, 128), HP)

    def send_next(h, n):
        part = (0, slice(None), pl.ds(h * H + n * HP, HP))
        return rcopy(
            zbuf.at[part],
            out_next.at[part],
            sz.at[0, h, n],
            rz.at[0, h, n],
            {"segment": lax.rem(seg + 1, n_seg)},
        )

    def send_prev(h, n):
        part = (slice(None), pl.ds(h * H + n * HP, HP))
        return rcopy(
            zbuf.at[(1,) + part],
            out_prev.at[(0,) + part],
            sz.at[1, h, n],
            rz.at[1, h, n],
            {"segment": lax.rem(seg - 1 + n_seg, n_seg)},
        )

    def emit_fwd(at):
        total = None
        for e in range(per):
            piece = mm(act[e], wd[e, :, pl.ds(at, H)])
            total = piece if total is None else total + piece
        return total

    def emit_bwd(at):
        total = None
        for e in range(per):
            for grads, w in ((gg, wg), (gu, wu)):
                piece = mm(grads[e], w[e, :, pl.ds(at, H)])
                total = piece if total is None else total + piece
        return total

    def finish_next(h, n, mixed):
        rows = X[0, k, j0, :, piece_cols(h, n)].astype(f32) + mixed
        zbuf[0, :, pl.ds(h * H + n * HP, HP)] = rows.astype(bf16)

        @pl.when(seg < n_seg - 1)
        def _():
            send_next(h, n).start()

    order = [*range(1, n_t), 0]

    def produce_all(r, emit, tag):
        pa = [None] * n_t
        pb = [None] * n_t
        qa = []
        qb = [None] * n_t
        for ti in range(1, n_t):
            with jax.named_scope(f"{tag}_a{ti}"):
                pa[ti] = produce(r, 0, ti, emit)
            with jax.named_scope(f"{tag}_b{ti}"):
                pb[ti] = produce(r, 1, ti, emit)
                qa.append(token_first(r, ti, pa[ti]))
        with jax.named_scope(f"{tag}_a0"):
            pa[0] = produce(r, 0, 0, emit)
            for ti in range(1, n_t):
                qb[ti] = expert_first(r, ti, pb[ti])
            token_rest(r, qa)
        with jax.named_scope(f"{tag}_b0"):
            pb[0] = produce(r, 1, 0, emit)
        return pa[0], pb[0], qa, qb

    with jax.named_scope("p07_norm"):
        c0[0].wait_recv()
        N[1 - k, j0] = normed_block(X[0, 1 - k, j0])[0]
    with jax.named_scope("p08_relay1"):
        for d, c in hops[0]:
            relay_first(0, d, c)
        relay_trail(0)
    with jax.named_scope("p09_relay2"):
        for d, c in hops[0]:
            relay_second(0, d, c)
            normalize_rows(0, k, d, c)
    with jax.named_scope("p10_arrive"):
        first_b = [h for h in hops[1] if h[1] == 0]
        later_b = [h for h in hops[1] if h[1] > 0]
        for d, c in first_b:
            relay_first(1, d, c)
        c0[1].wait_recv()
        N2[1 - k, j0] = normed_block(X[1, 1 - k, j0])[0]
        all_gates.wait_recv()
        turn[...] = jnp.zeros((128, 128), f32)
        for p in range(2):
            for j in range(J):
                turn[0 : 2 * E] = GT[p * J + j]
                G[p, j] = jnp.transpose(turn[...])[0:tok]
        arrive_trail(0)
        for d, c in hops[0]:
            arrive(0, d, c)
            normalize_rows(0, 1 - k, d, c)
        for d, c in later_b:
            relay_first(1, d, c)

    with jax.named_scope("p11_fwd0"):
        weights[0][0].wait()
        weights[1][0].wait()
        fwd_part(0)
    with jax.named_scope("p12_relay"):
        for d, c in hops[2]:
            relay_first(2, d, c)
    with jax.named_scope("p13_fwd1"):
        for e in range(1, per):
            weights[0][e].wait()
            weights[1][e].wait()
            fwd_part(e)
        for e in range(per):
            weights[2][e].wait()
    with jax.named_scope("p13b_relay"):
        for d, c in first_b:
            relay_second(1, d, c)
        relay_trail(1)
        relay_trail(2)
    with jax.named_scope("p14_prod"):
        pa = []
        pb = []
        for ti in order[:-1]:
            pa.append(produce(0, 0, ti, emit_fwd))
            pb.append(produce(0, 1, ti, emit_fwd))
        for d, c in later_b:
            relay_second(1, d, c)
        pa.append(produce(0, 0, 0, emit_fwd))
        for d, c in hops[2]:
            relay_second(2, d, c)
        pb.append(produce(0, 1, 0, emit_fwd))
    with jax.named_scope("p14z_relay"):
        arrive_trail(1)
        for d, c in hops[1]:
            arrive(1, d, c)
        for d in range(1, J):
            src = lax.rem(j0 - d + J, J)
            for p in range(2):
                N2[p, src] = normed_block(X[1, p, src])[0]
    with jax.named_scope("p16_first"):
        qa = [token_first(0, ti, pa[n]) for n, ti in enumerate(order[:-1])]
        qb = [None] * n_t
        for n, ti in enumerate(order[:-1]):
            qb[ti] = expert_first(0, ti, pb[n])
        token_rest(0, qa)
    with jax.named_scope("p16b_cot"):
        c0[2].wait_recv()
        arrive_trail(2)
        for d, c in hops[2]:
            arrive(2, d, c)
    with jax.named_scope("p17_bwd"):
        for e in range(per):
            bwd_part(e)
    with jax.named_scope("p18_fsec"):
        za = then_expert(0, pa[-1], qa)
        zb = [then_token(0, ti, qb[ti]) for ti in range(1, n_t)]
        qb[0] = expert_first(0, 0, pb[-1])

    with jax.named_scope("p19_sendS"):
        flipped = jnp.transpose(Sc[...])[0:8]
        for p in range(2):
            for j in range(J):
                at = (p * J + j) * tok
                Sb[j * 2 + p] = flipped[:, at : at + tok]
        for de in range(n_e):
            for dt in range(n_t):
                if de or dt:
                    to = lax.rem(me + de, n_e)
                    piece(
                        rcopy(
                            Sb.at[to],
                            RS.at[me * n_t + x],
                            sS.at[0],
                            rS.at[0],
                            {"expert": to, "token": lax.rem(x + dt, n_t)},
                        )
                    )
        blocks = RS.at[pl.ds(0, n_e * n_t - 1)]
        all_sums = rcopy(blocks, blocks, sS.at[0], rS.at[0], {"expert": sib})
        started.append(all_sums)
        RS[me * n_t + x] = Sb[me]

    qa0, zb0 = qa, zb
    pa, pb, qa, qc = produce_all(1, emit_bwd, "p20_prod")
    with jax.named_scope("p21_first"):
        zc = then_expert(1, pa, qa)
    with jax.named_scope("p23_dgt"):
        all_sums.wait_recv()
        DGT[...] = jnp.zeros(DGT.shape, f32)
        corr = jnp.zeros((1, tok), f32)
        for e in range(n_e):
            total = RS[e * n_t]
            for t in range(1, n_t):
                total += RS[e * n_t + t]
            DGT[e * per : (e + 1) * per, 0:tok] = total[0:per]
            corr += total[per : per + 1]
        DGT[E : E + 1, 0:tok] = corr
        turned = jnp.transpose(DGT[...])[0:tok]
        logits_b = own[0, :, 0:E]
        probs_b = own[1, :, 0:E]
        total_b = own[4, :, 0:E]
        inverse_b = own[5, :, 0:1]
        dgates = jnp.where(own[3, :, 0:E] > 0.5, turned[:, 0:E], 0.0)
        spread = jnp.sum(dgates * probs_b, axis=-1, keepdims=True)
        dprobs = route_scale * dgates / total_b - route_scale * spread / (total_b * total_b)
        dlogits = jnp.where(own[2, :, 0:E] > 0.5, dprobs * probs_b * (1.0 - probs_b), 0.0)
        mean_all = (turned[:, E : E + 1] + jnp.sum(dlogits * logits_b, axis=-1, keepdims=True)) / D
        router_own = lax.dot_general(
            dlogits, router_t[:, cols(x)], NN, precision=highest, preferred_element_type=f32
        )
        gain_own = gain[:, cols(x)]
        scaled_own = X[1, k, j0, :, cols(x)].astype(f32) * inverse_b
        cot_own = X[2, k, j0, :, cols(x)].astype(f32)
        base = cot_own + inverse_b * (router_own * gain_own - scaled_own * mean_all)
        scale_own = inverse_b * gain_own
        own_base[0] = base
        own_base[1] = scale_own
        qc[0] = expert_first(1, 0, pb)

    with jax.named_scope("p24_second"):
        zb = [then_token(1, ti, qc[ti]) for ti in range(1, n_t)]

    with jax.named_scope("p22_finnext"):
        for n in range(NP):
            finish_next(0, n, last_a(0, n, qa0, za))
        for n in range(NP):
            finish_next(1, n, last_b(0, n, qb[0], zb0))

        @pl.when(seg == 0)
        def _():
            out_next[...] = jnp.zeros(out_next.shape, bf16)

        @pl.when(seg == n_seg - 1)
        def _():
            out_prev[...] = jnp.zeros(out_prev.shape, bf16)

    def finish_prev(h, n, mixed):
        at = slice(h * H + n * HP, h * H + (n + 1) * HP)
        zbuf[1, :, at] = (own_base[0, :, at] + own_base[1, :, at] * mixed).astype(bf16)

        @pl.when(seg > 0)
        def _():
            send_prev(h, n).start()

    with jax.named_scope("p25_lasta"):
        for n in range(NP):
            finish_prev(0, n, last_a(1, n, qa, zc))
    with jax.named_scope("p26_lastb"):
        for n in range(NP):
            finish_prev(1, n, last_b(1, n, qc[0], zb))

    with jax.named_scope("p27_end"):
        for c in started:
            c.wait_send()

        @pl.when(seg < n_seg - 1)
        def _():
            for h, n in pieces:
                send_next(h, n).wait_send()
                send_prev(h, n).wait_recv()

        @pl.when(seg > 0)
        def _():
            for h, n in pieces:
                send_prev(h, n).wait_send()
                send_next(h, n).wait_recv()


def settle(next_in, prev_in, next_out, prev_out):
    next_out[...] = next_in[...]
    prev_out[...] = prev_in[...]


def body(
    fwd_acts,
    fwd_ids,
    fwd_slots,
    bwd_acts,
    bwd_ids,
    bwd_slots,
    bwd_grad,
    norm_gain,
    router,
    w_gate,
    w_up,
    w_down,
):
    E = router.shape[2]
    per, D, F = w_gate.shape
    n_seg = lax.axis_size("segment")
    n_e = lax.axis_size("expert")
    n_t = lax.axis_size("token")
    tok = fwd_acts.shape[1]
    K = fwd_ids.shape[2]
    cap = max(2, min(3 * tok * K // (4 * E), tok - 1))
    W = D // n_t
    J = n_e // 2
    T = n_e * tok
    V = pltpu.VMEM
    dma = pltpu.SemaphoreType.DMA
    peers = max(J - 1, 1)
    CH = tuple(max(n // peers, 1) for n in (4, 2, 1))
    toks = max(n_t - 1, 1)
    scratch = [
        V((3, 2, J, tok, D), bf16),
        V((2, J, tok, D), bf16),
        V((2, J, tok, D), bf16),
        V((2, J, tok, 128), f32),
        V((n_e, 2 * E, 128), f32),
        V((per, F, D), bf16),
        V((per, F, D), bf16),
        V((per, F, D), bf16),
        V((per, T, F), bf16),
        V((per, T, F), bf16),
        V((per, T, F), bf16),
        V((2, 2, 2, n_t, J, tok, W // 2), bf16),
        V((2, 2, n_t, J, tok, W // 2), bf16),
        V((2, toks, J, tok, W // 2), bf16),
        V((2, toks, J, tok, W // 2), bf16),
        V((2, peers, tok, W // 2), bf16),
        V((2, peers, tok, W // 2), bf16),
        V((2, peers, n_t, tok, W // 2), bf16),
        V((2, peers, n_t, tok, W // 2), bf16),
        V((2, n_t, tok, W // 2), bf16),
        V((2, toks, tok, W // 2), bf16),
        V((T, 128), f32),
        V((n_e, 8, tok), f32),
        V((n_e * n_t, 8, tok), f32),
        V((128, 128), f32),
        V((6, tok, 128), f32),
        V((2, tok, W), f32),
        V((2, tok, W), bf16),
        V((128, 128), f32),
        V((4, K, 1, tok), jnp.int32),
        V((1, D), f32),
        V((E, D), f32),
        dma((3, per)),
        dma((2,)),
        dma((3,)),
        dma((1,)),
        dma((3,)),
        dma((peers,)),
        dma((peers, sum(CH))),
        dma((peers, 3)),
        dma((1,)),
        dma((1,)),
        dma((peers,)),
        dma((peers, sum(CH))),
        dma((peers, 3)),
        dma((peers, toks)),
        dma((peers, toks, sum(CH))),
        dma((1,)),
        dma((2, 2, n_t)),
        dma((1,)),
        dma((2, toks, 4)),
        dma((1,)),
        dma((2, peers, 2)),
        dma((1,)),
        dma((2, peers, n_t, 2)),
        dma((1,)),
        dma((2, toks, 2)),
        dma((1,)),
        dma((1,)),
        dma((2, 2, 2)),
        dma((2, 2, 2)),
    ]
    held = sum(
        int(np.prod(s.shape)) * jnp.dtype(s.dtype).itemsize
        for s in scratch
        if s.memory_space == V
    )
    vm = pl.BlockSpec(memory_space=pltpu.VMEM)
    hbm = pl.BlockSpec(memory_space=pltpu.HBM)
    out = jax.ShapeDtypeStruct((1, tok, W), bf16)
    sizes = (n_seg, n_e, n_t, per, E, tok, D, F, K, CH, cap)
    moved = pl.pallas_call(
        functools.partial(kernel, sizes),
        out_shape=(out, out),
        in_specs=[hbm] * 12,
        out_specs=(vm, vm),
        scratch_shapes=scratch,
        compiler_params=pltpu.CompilerParams(
            collective_id=0, has_side_effects=True, vmem_limit_bytes=held + 9 * 1024 * 1024
        ),
        name="relay_moe",
    )(
        *(
            pltpu.with_memory_space_constraint(t, pltpu.HBM)
            for t in (
                fwd_acts,
                bwd_acts,
                bwd_grad,
                *(jnp.transpose(t, (2, 0, 1)) for t in (fwd_ids, fwd_slots, bwd_ids, bwd_slots)),
                norm_gain,
                router[0].T,
                jnp.swapaxes(w_gate, 1, 2),
                jnp.swapaxes(w_up, 1, 2),
                w_down,
            )
        )
    )
    return pl.pallas_call(
        settle, out_shape=(out, out), in_specs=[vm] * 2, out_specs=(vm, vm), name="settle",
        compiler_params=pltpu.CompilerParams(vmem_limit_bytes=2 * 1024 * 1024),
    )(*moved)


def solution(mesh):
    return jax.shard_map(
        body,
        mesh=mesh,
        in_specs=(
            P("segment", "expert", None),
            P("segment", "expert", None),
            P("segment", "expert", None),
            P("segment", "expert", None),
            P("segment", "expert", None),
            P("segment", "expert", None),
            P("segment", "expert", None),
            P("segment", None),
            P("segment", None, None),
            P("expert", None, "token"),
            P("expert", None, "token"),
            P("expert", "token", None),
        ),
        out_specs=(P("segment", "expert", "token"), P("segment", "expert", "token")),
        check_vma=False,
    )
```
